512 devices in a mesh: rep: 32 (over y, x, core), tp: 16 (over z).
Axes of the slice: x: 4, y: 4, z: 16, core: 2. Of those that a mesh axis runs over, the one named last changes fastest.
Arguments:
- tokens: bfloat16 [512, 1024], P('rep'), may hold values from -6 to 6
- lengths: int32 [512], P('rep'), may hold values from 1 to 256, as said below
- prompt_group: int32 [512], P('rep'), may hold values from 0 to 7
- span_close: int32 [512], P('rep'), may hold values 0 or 1
- out_slot: int32 [32, 2], P('rep'), may hold values from 0 to 15, as said below
- move_dest: int32 [32, 2], P('rep'), may hold values from 0 to 31, as said below
- page_table: int32 [512, 2, 1], P('rep'), may hold values from 0 to 15, as said below
- cache_pool: bfloat16 [512, 16, 128, 256], P('rep', 'tp'), may hold values from -6 to 6
- prefix_cache: bfloat16 [8, 16, 64, 256], P(None, 'tp'), may hold values from -6 to 6
- memory: float32 [512, 16, 64, 128], P('rep', 'tp'), may hold values from -2 to 2
- norm_attn: float32 [1024], replicated, may hold values from 0.5 to 1.5
- norm_mlp: float32 [1024], replicated, may hold values from 0.5 to 1.5
- qkv_weight: bfloat16 [1024, 3072], P(None, 'tp'), may hold values from -0.1875 to 0.1875
- out_weight: bfloat16 [1024, 1024], P('tp'), may hold values from -0.1875 to 0.1875
- gate_weight: bfloat16 [1024, 2816], P(None, 'tp'), may hold values from -0.1875 to 0.1875
- up_weight: bfloat16 [1024, 2816], P(None, 'tp'), may hold values from -0.1875 to 0.1875
- down_weight: bfloat16 [2816, 1024], P('tp'), may hold values from -0.109375 to 0.109375
- forget: float32 [8], replicated, may hold values from 0.5 to 0.99
- write_rate: float32 [8], replicated, may hold values from 0.1 to 0.9
Outputs:
- out_rows: bfloat16 [512, 1024], P('rep')
- new_memory: float32 [512, 16, 64, 128], P('rep', 'tp')
- new_cache_pool: bfloat16 [512, 16, 128, 256], P('rep', 'tp')
The draws below stay inside these ranges and needn't reach their ends.
Inputs may be any that keep to these rules, and one draw needn't show every extreme that they name: `lengths`: the cached tokens of a request; some request of every replica holds 256. `out_slot`: the 2 slots of one replica are distinct. For each m, move_dest[:, m] is a permutation of the replicas. `page_table`: for each replica and half, the entries of its 16 slots are a permutation of 0 to 15.
All inputs are finite; a program needn't handle non-finite values. No bound on the sum of `span_close` on one device may be relied on, other than what follows from the above.
Results may differ from the reference program's by a relative error of at most 0.013.
Values may be sent and summed in bfloat16 or wider, within the bound.
No kernel may reach another device: no remote copies, remote signals or barrier semaphores. Data moves between devices by JAX's collectives and lax.ppermute only.
A program may use at most 64 MiB of HBM per device.

```python
import jax
import jax.numpy as jnp
from jax import lax

D = 1024
HEADS = 8
HEAD = 128
FF = 2816
PAGE = 128
HP = 1
PREFIX = 128
GROUPS = 8
MOVES = 2
REQ_DEV = 16
REQUESTS = 512
POOL = 16
SECTIONS = 16
N_REP = 32


def draw_lengths(key, part):
    values = jax.random.randint(key, (REQUESTS,), 1, 2 * HP * PAGE + 1)
    return values.at[::REQ_DEV].set(2 * HP * PAGE).astype(jnp.int32)


def draw_out_slot(key, part):
    keys = jax.random.split(key, N_REP)
    rows = jax.vmap(lambda single: jax.random.permutation(single, REQ_DEV)[:MOVES])(keys)
    return rows.astype(jnp.int32)


def draw_move_dest(key, part):
    keys = jax.random.split(key, MOVES)
    columns = jax.vmap(lambda single: jax.random.permutation(single, N_REP))(keys)
    return columns.T.astype(jnp.int32)


def draw_page_table(key, part):
    keys = jax.random.split(key, N_REP * 2)
    perms = jax.vmap(lambda single: jax.random.permutation(single, REQ_DEV * HP))(keys)
    perms = perms.reshape(N_REP, 2, REQ_DEV, HP).transpose(0, 2, 1, 3)
    return perms.reshape(REQUESTS, 2, HP).astype(jnp.int32)


def touch_ends(drawn, stream_key, smallest, largest):
    longest = drawn.shape.index(max(drawn.shape))
    spots = []
    for shift in (0, 1):
        where = [jax.random.randint(jax.random.fold_in(stream_key, axis), (), 0, length) for axis, length in enumerate(drawn.shape)]
        where[longest] = (where[longest] + shift) % drawn.shape[longest]
        spots.append(tuple(where))
    return drawn.at[spots[0]].set(smallest).at[spots[1]].set(largest)


def block_scale(rng, extent, pieces, least, high):
    loudness = 1.0
    for axis_at, shards_of in pieces:
        draws = jax.random.uniform(jax.random.fold_in(jax.random.fold_in(rng, 6), axis_at), (shards_of,), jnp.float32, least / len(pieces), high / len(pieces))
        loudness = loudness * jnp.repeat(jnp.exp(draws), extent[axis_at] // shards_of).reshape((-1,) + (1,) * (len(extent) - 1 - axis_at))
    return loudness


def scatter_about(own_key, dims, width, bound, cuts=(), dtype=jnp.bfloat16):
    gain = block_scale(own_key, dims, cuts, -0.22, 0.18) if cuts else 1.0
    values = jax.random.normal(own_key, dims, jnp.float32) * width * gain
    return jnp.minimum(jnp.maximum(values, -bound), bound).astype(dtype)


def setup_inputs(seed: int = 0) -> dict:
    splits = jax.random.split(jax.random.key(seed), 20)
    tokens = scatter_about(splits[0], (REQUESTS, D), 1.0, 6.0, ((0, 32),))
    lengths = draw_lengths(jax.random.fold_in(splits[19], 71), 0)
    prompt_group = touch_ends(jax.random.randint(splits[2], (REQUESTS,), 0, GROUPS), jax.random.fold_in(splits[2], 1), 0, GROUPS - 1).astype(jnp.int32)
    span_close = touch_ends((jax.random.randint(splits[3], (REQUESTS,), 0, 2) < 1).astype(jnp.int32), jax.random.fold_in(splits[3], 1), 0, 1)
    out_slot = draw_out_slot(jax.random.fold_in(splits[19], 71), 0)
    move_dest = draw_move_dest(jax.random.fold_in(splits[19], 71), 0)
    page_table = draw_page_table(jax.random.fold_in(splits[19], 71), 0)
    cache_pool = scatter_about(splits[7], (N_REP * POOL, SECTIONS, PAGE, 2 * HEAD), 1.0, 6.0, ((0, 32), (1, 16)))
    prefix_cache = scatter_about(splits[8], (GROUPS, SECTIONS, PREFIX // 2, 2 * HEAD), 1.0, 6.0, ((1, 16),))
    memory = scatter_about(splits[9], (REQUESTS, SECTIONS, HEAD // 2, HEAD), 0.3, 2.0, ((0, 32), (1, 16)), jnp.float32)
    norm_attn = jnp.clip(1.0 + 0.1 * jax.random.normal(splits[10], (D,), jnp.float32), 0.5, 1.5)
    norm_mlp = jnp.clip(1.0 + 0.1 * jax.random.normal(splits[11], (D,), jnp.float32), 0.5, 1.5)
    qkv_weight = scatter_about(splits[12], (D, 3 * D), D ** -0.5, 0.1875, ((1, 16),))
    out_weight = scatter_about(splits[13], (D, D), D ** -0.5, 0.1875, ((0, 16),))
    gate_weight = scatter_about(splits[14], (D, FF), D ** -0.5, 0.1875, ((1, 16),))
    up_weight = scatter_about(splits[15], (D, FF), D ** -0.5, 0.1875, ((1, 16),))
    down_weight = scatter_about(splits[16], (FF, D), FF ** -0.5, 0.109375, ((0, 16),))
    forget = jnp.clip(jax.random.uniform(splits[17], (HEADS,), jnp.float32, 0.5, 0.99), 0.5, 0.99)
    write_rate = jnp.clip(jax.random.uniform(splits[18], (HEADS,), jnp.float32, 0.1, 0.9), 0.1, 0.9)
    return {"tokens": tokens, "lengths": lengths, "prompt_group": prompt_group, "span_close": span_close, "out_slot": out_slot, "move_dest": move_dest, "page_table": page_table, "cache_pool": cache_pool, "prefix_cache": prefix_cache, "memory": memory, "norm_attn": norm_attn, "norm_mlp": norm_mlp, "qkv_weight": qkv_weight, "out_weight": out_weight, "gate_weight": gate_weight, "up_weight": up_weight, "down_weight": down_weight, "forget": forget, "write_rate": write_rate}


highest = lax.Precision.HIGHEST

def rms_scale(values, gain_vec):
    return values * lax.rsqrt(lax.optimization_barrier(jnp.mean(values * values, axis=-1, keepdims=True)) + 1e-05) * gain_vec

def unit_rows(values):
    return values * lax.rsqrt(lax.optimization_barrier(jnp.sum(values * values, axis=-1, keepdims=True)) + 1e-06)

def reference(tokens, lengths, prompt_group, span_close, out_slot, move_dest, page_table, cache_pool, prefix_cache, memory, norm_attn, norm_mlp, qkv_weight, out_weight, gate_weight, up_weight, down_weight, forget, write_rate):
    residual_in = tokens.astype(jnp.float32)
    normed = rms_scale(residual_in, norm_attn).astype(jnp.bfloat16)
    qkv_full = jnp.dot(normed, qkv_weight, preferred_element_type=jnp.float32).astype(jnp.bfloat16)
    queries = qkv_full[:, :D].reshape(REQUESTS, HEADS, HEAD).astype(jnp.float32)
    keys_new = qkv_full[:, D:2 * D].reshape(REQUESTS, HEADS, HEAD).astype(jnp.float32)
    values_new = qkv_full[:, 2 * D:].reshape(REQUESTS, HEADS, HEAD).astype(jnp.float32)
    score_scale = HEAD ** (-0.5)
    positions = ((2 * jnp.arange(HP)[None, :, None] + jnp.arange(2)[:, None, None]) * PAGE + jnp.arange(PAGE)[None, None, :]).reshape(-1)
    sect_half = jnp.arange(2 * HEADS) // HEADS

    def one_replica(inputs):
        pool_rows, table_rows, query_rows, key_rows, value_rows, length_rows, group_ids = inputs
        page_data = pool_rows[table_rows[:, sect_half, :], jnp.arange(2 * HEADS)[None, :, None]]
        page_data = page_data.reshape(REQ_DEV, 2, HEADS, HP * PAGE, 2 * HEAD).transpose(0, 2, 1, 3, 4)
        page_data = page_data.reshape(REQ_DEV, HEADS, 2 * HP * PAGE, 2 * HEAD).astype(jnp.float32)
        prefix = prefix_cache[group_ids].reshape(REQ_DEV, 2, HEADS, PREFIX // 2, 2 * HEAD).transpose(0, 2, 1, 3, 4)
        prefix = prefix.reshape(REQ_DEV, HEADS, PREFIX, 2 * HEAD).astype(jnp.float32)
        key_data = jnp.concatenate([prefix, page_data], axis=2)
        live_keys = jnp.concatenate([jnp.ones((REQ_DEV, PREFIX), bool), positions[None, :] < length_rows[:, None]], axis=1)[:, None, :]
        scores = jnp.einsum('rhd,rhnd->rhn', query_rows, key_data[..., :HEAD], precision=highest) * score_scale
        scores = jnp.where(live_keys, scores, -jnp.inf)
        own_score = lax.optimization_barrier(jnp.sum(query_rows * key_rows, axis=-1)) * score_scale
        top_score = jnp.maximum(lax.optimization_barrier(jnp.max(scores, axis=-1)), own_score)
        weights = jnp.exp(scores - top_score[..., None])
        own_weight = jnp.exp(own_score - top_score)
        denom_sum = lax.optimization_barrier(jnp.sum(weights, axis=-1)) + own_weight
        accumulated = jnp.einsum('rhn,rhnd->rhd', weights, key_data[..., HEAD:], precision=highest) + own_weight[..., None] * value_rows
        return accumulated / denom_sum[..., None]
    attended = lax.map(one_replica, (cache_pool.reshape(N_REP, POOL, 2 * HEADS, PAGE, 2 * HEAD), page_table.reshape(N_REP, REQ_DEV, 2, HP), queries.reshape(N_REP, REQ_DEV, HEADS, HEAD), keys_new.reshape(N_REP, REQ_DEV, HEADS, HEAD), values_new.reshape(N_REP, REQ_DEV, HEADS, HEAD), lengths.reshape(N_REP, REQ_DEV), prompt_group.reshape(N_REP, REQ_DEV))).reshape(REQUESTS, HEADS, HEAD)
    query_unit = unit_rows(queries)
    key_unit = unit_rows(keys_new)
    mem_full = memory.reshape(REQUESTS, 2, HEADS, HEAD // 2, HEAD).transpose(0, 2, 1, 3, 4).reshape(REQUESTS, HEADS, HEAD, HEAD)
    recalled = jnp.einsum('rhij,rhj->rhi', mem_full, query_unit, precision=highest)
    mixed_sum = (attended + recalled).reshape(REQUESTS, HEADS, 2, HEAD // 2).transpose(0, 2, 1, 3)
    mixed_out = mixed_sum.reshape(REQUESTS, D).astype(jnp.bfloat16)
    hidden_in = residual_in + jnp.dot(mixed_out, out_weight, preferred_element_type=jnp.float32)
    normed_mlp = rms_scale(hidden_in, norm_mlp).astype(jnp.bfloat16)
    gate_out = jnp.dot(normed_mlp, gate_weight, preferred_element_type=jnp.float32)
    up_out = jnp.dot(normed_mlp, up_weight, preferred_element_type=jnp.float32)
    activated = (jax.nn.silu(gate_out) * up_out).astype(jnp.bfloat16)
    rows_done = (hidden_in + jnp.dot(activated, down_weight, preferred_element_type=jnp.float32)).astype(jnp.bfloat16)
    predicted = jnp.einsum('rhij,rhj->rhi', mem_full, key_unit, precision=highest)
    misfit = values_new - predicted
    updated = forget[None, :, None, None] * mem_full + write_rate[None, :, None, None] * misfit[..., None] * key_unit[:, :, None, :]
    mem_after = jnp.where(span_close[:, None, None, None] == 1, updated, mem_full)
    mem_after = mem_after.reshape(REQUESTS, HEADS, 2, HEAD // 2, HEAD).transpose(0, 2, 1, 3, 4).reshape(memory.shape)
    src_rows = (jnp.arange(N_REP)[:, None] * REQ_DEV + out_slot).astype(jnp.int32)
    dst_rows = (move_dest * REQ_DEV + out_slot[move_dest, jnp.arange(MOVES)[None, :]]).astype(jnp.int32)
    new_from = jnp.arange(REQUESTS).astype(jnp.int32).at[dst_rows.reshape(-1)].set(src_rows.reshape(-1))
    src_pages = (jnp.arange(N_REP)[:, None, None, None] * POOL + page_table[src_rows][:, :, sect_half, :]).astype(jnp.int32)
    dst_pages = (move_dest[:, :, None, None] * POOL + page_table[dst_rows][:, :, sect_half, :]).astype(jnp.int32)
    sect_ids = jnp.arange(2 * HEADS).astype(jnp.int32)[None, None, :, None]
    new_pool = cache_pool.at[dst_pages, sect_ids].set(cache_pool[src_pages, sect_ids])
    return (rows_done[new_from], mem_after[new_from], new_pool)
```

```python
import jax
import jax.numpy as jnp
from jax import lax
from jax.experimental import pallas as pl
from jax.experimental.pallas import tpu as pltpu
from jax.sharding import PartitionSpec as P

f32 = jnp.float32
bf16 = jnp.bfloat16
highest = lax.Precision.HIGHEST
LANES = 128

VMEM = pl.BlockSpec(memory_space=pltpu.VMEM)
SMEM = pl.BlockSpec(memory_space=pltpu.SMEM)
HBM = pl.BlockSpec(memory_space=pl.ANY)


def call(kernel, outs, in_specs, out_specs=None, scratch=(), aliases=None):
    return pl.pallas_call(
        kernel,
        out_shape=outs,
        in_specs=in_specs,
        out_specs=out_specs if out_specs is not None else jax.tree.map(lambda _: VMEM, outs),
        scratch_shapes=scratch,
        input_output_aliases=aliases or {},
        compiler_params=pltpu.CompilerParams(vmem_limit_bytes=48 << 20),
    )


def lane_ids(shape):
    return lax.broadcasted_iota(jnp.int32, shape, len(shape) - 1)


def row_ids(shape):
    return lax.broadcasted_iota(jnp.int32, shape, len(shape) - 2)


def column(values, count, lanes=LANES):
    rows = row_ids((count, lanes))
    out = jnp.zeros((count, lanes), jnp.int32)
    for r in range(count):
        out = jnp.where(rows == r, values[r], out)
    return out


def half_swap(block):
    return pltpu.roll(block, LANES // 2, 1)


def qkv_kernel(tokens, gain, weight, out):
    t = lax.axis_index("tp")
    x = tokens[...].astype(f32)
    scale = lax.rsqrt(jnp.mean(x * x, axis=-1, keepdims=True) + 1e-05)
    normed = (x * scale * gain[...]).astype(bf16)
    part = jnp.dot(normed, weight[...], preferred_element_type=f32)
    part = part.astype(bf16).astype(f32)
    first = part[:, :LANES]
    last = part[:, LANES:]
    turned = half_swap(first)
    lanes = lane_ids(first.shape)
    low = lanes < 64
    blocks = (
        jnp.where(low, first, turned),
        jnp.where(low, turned, first),
        jnp.concatenate([last, last], axis=1),
    )
    placed = []
    for j, block in enumerate(blocks):
        sub = lax.rem(3 * t + j, 2)
        placed.append(jnp.where(lanes // 64 == sub, block, 0.0))
    for head in range(8):
        slot = jnp.zeros(first.shape, f32)
        for j in range(3):
            mine = lax.rem(3 * t + j, 16) // 2 == head
            slot = slot + jnp.where(mine, placed[j], 0.0)
        out[head] = slot.astype(bf16)
        out[head + 8] = slot.astype(bf16)


def attend_kernel(
    lengths, groups, span, pages, slots, forget, rate,
    recv, pool, prefix, memory, own_weight, pair_weight,
    terms_out, memory_out, send_out,
    masked, terms,
):
    t = lax.axis_index("tp")
    half = t // 8
    head = lax.rem(t, 8)

    def pick(kind):
        one = (16 * kind + 2 * head) // 3
        two = (16 * kind + 2 * head + 1) // 3
        a = recv[one].astype(f32)
        b = recv[two].astype(f32)
        return jnp.where(one == two, a, a + b)

    query = pick(0)
    key = pick(1)
    value = pick(2)
    rows = query.shape[0]
    shape = (rows, LANES)
    lanes = lane_ids(shape)
    row = row_ids(shape)
    low = lanes < 64
    length = column(lengths, rows)
    group = column(groups, rows)
    page = jnp.zeros(shape, jnp.int32)
    for r in range(rows):
        page = jnp.where(row == r, pages[2 * r + half], page)

    score_scale = LANES ** (-0.5)
    nt = (((1,), (1,)), ((), ()))
    page_count = pool.shape[0]
    query_b = query.astype(bf16)
    pool_keys = pool[:, :, :LANES].reshape(page_count * LANES, LANES)
    pool_scores = lax.dot_general(query_b, pool_keys, nt, preferred_element_type=f32)
    pre_rows = prefix.shape[0] * prefix.shape[1]
    pre_keys = prefix[:, :, :LANES].reshape(pre_rows, LANES)
    pre_scores = lax.dot_general(query_b, pre_keys, nt, preferred_element_type=f32)
    tiles = []
    in_reach = lanes + half * LANES < length
    for p in range(page_count):
        live = (page == p) & in_reach
        tile = pool_scores[:, p * LANES : (p + 1) * LANES] * score_scale
        tiles.append(jnp.where(live, tile, -jnp.inf))
    for p in range(pre_rows // LANES):
        live = group == lanes // 64 + 2 * p
        tile = pre_scores[:, p * LANES : (p + 1) * LANES] * score_scale
        tiles.append(jnp.where(live, tile, -jnp.inf))
    own = jnp.sum(query * key, axis=-1, keepdims=True) * score_scale
    own = jnp.where(half == 0, own, -jnp.inf)
    peak = tiles[0]
    for tile in tiles[1:]:
        peak = jnp.maximum(peak, tile)
    top = jnp.maximum(jnp.max(peak, axis=-1, keepdims=True), own)
    weights = [jnp.exp(tile - top) for tile in tiles]
    own_weight_ = jnp.exp(own - top)
    total = weights[0]
    for tile in weights[1:]:
        total = total + tile
    denom = jnp.sum(total, axis=-1, keepdims=True) + own_weight_

    def both(parts):
        full = jnp.concatenate(parts, axis=1)
        upper = full.astype(bf16)
        lower = (full - upper.astype(f32)).astype(bf16)
        return jnp.concatenate([upper, lower], axis=0)

    pool_values = pool[:, :, LANES:].reshape(page_count * LANES, LANES)
    pre_values = prefix[:, :, LANES:].reshape(pre_rows, LANES)
    summed = jnp.dot(both(weights[:page_count]), pool_values, preferred_element_type=f32)
    summed = summed + jnp.dot(
        both(weights[page_count:]), pre_values, preferred_element_type=f32
    )
    summed = summed[:rows] + summed[rows:] + own_weight_ * value
    attended = summed / denom
    lse = top + jnp.log(denom)

    query_unit = query * lax.rsqrt(jnp.sum(query * query, axis=-1, keepdims=True) + 1e-06)
    key_unit = key * lax.rsqrt(jnp.sum(key * key, axis=-1, keepdims=True) + 1e-06)
    mem_rows = memory.shape[1]
    flat_memory = memory[...].reshape(rows * mem_rows, LANES)
    seen = lax.dot_general(
        jnp.concatenate([query_unit, key_unit], axis=0), flat_memory, nt,
        preferred_element_type=f32, precision=highest,
    )
    recalled = jnp.zeros(shape, f32)
    value_half = jnp.where(half == 0, value, half_swap(value))
    value_both = jnp.where(low, value_half, half_swap(value_half))
    closing = column(span, rows) == 1
    step = rate[head]
    keep = forget[head]
    for c in range(rows // 2):
        mine = row == 2 * c + lanes // 64
        cut = slice(c * LANES, (c + 1) * LANES)
        recalled = recalled + jnp.where(mine, seen[:rows, cut], 0.0)
        misfit = (value_both - seen[rows:, cut]) * step
        masked[:, cut] = jnp.where(mine & closing, misfit, 0.0)
    recalled = recalled + half_swap(recalled)
    change = lax.dot_general(
        masked[...], key_unit, (((0,), (0,)), ((), ())),
        preferred_element_type=f32, precision=highest,
    )
    for r in range(rows):
        decay = jnp.where(span[r] == 1, keep, 1.0)
        memory_out[r] = decay * memory[r] + change[r * mem_rows : (r + 1) * mem_rows]

    for m in range(2):
        slot = slots[0, m]
        send_out[m * LANES : (m + 1) * LANES, :] = pool[pages[2 * slot + half]]
        send_out[2 * LANES :, m * LANES : (m + 1) * LANES] = memory_out[slot].astype(bf16)

    turned = jnp.where(half == 0, attended, half_swap(attended))
    left = jnp.concatenate([turned, jnp.where(low, recalled, 0.0)], axis=0).astype(bf16)
    right = jnp.concatenate([own_weight[...], pair_weight[...]], axis=0)
    projected = jnp.dot(left, right, preferred_element_type=f32)
    for k in range(8):
        terms[:, k, :] = projected[:rows, k * LANES : (k + 1) * LANES]
        terms[:, k + 8, :] = projected[rows:, k * LANES : (k + 1) * LANES]
    one = lse.astype(bf16).astype(f32)
    two = (lse - one).astype(bf16).astype(f32)
    terms[:, 16, :] = jnp.broadcast_to(one, shape)
    terms[:, 17, :] = jnp.broadcast_to(two, shape)
    terms[:, 18, :] = jnp.broadcast_to(lse - one - two, shape)
    for k in range(19, 24):
        terms[:, k, :] = jnp.zeros(shape, f32)
    terms_out[...] = terms[...].astype(bf16)


def hidden_kernel(recv, tokens, gain, hidden_out, normed_out, terms):
    t = lax.axis_index("tp")
    terms[...] = recv[...].astype(f32)
    lse = terms[:, 16, :] + terms[:, 17, :] + terms[:, 18, :]
    count = lse.shape[0]
    other = jnp.concatenate([lse[count // 2 :], lse[: count // 2]], axis=0)
    share = 1.0 / (1.0 + jnp.exp(other - lse))
    x = tokens[...].astype(f32)
    x = jnp.sum(jnp.where(row_ids(x.shape) == t, x, 0.0), axis=0, keepdims=True)
    parts = []
    for k in range(8):
        part = share * terms[:, k, :] + terms[:, k + 8, :]
        part = jnp.sum(part, axis=0, keepdims=True)
        parts.append(part + x[:, k * LANES : (k + 1) * LANES])
    hidden = jnp.concatenate(parts, axis=0)
    hidden_out[...] = hidden
    square = jnp.sum(jnp.sum(hidden * hidden, axis=1, keepdims=True), axis=0, keepdims=True)
    scale = lax.rsqrt(square / (8 * LANES) + 1e-05)
    normed = (hidden * scale * gain[...]).astype(bf16)
    for s in range(16):
        normed_out[s] = normed


def mlp_kernel(recv, gate_weight, up_weight, down_weight, out, rows):
    rows[...] = recv[...].astype(f32)
    x = jnp.concatenate([rows[:, k, :] for k in range(8)], axis=1).astype(bf16)
    gate = jnp.dot(x, gate_weight[...], preferred_element_type=f32)
    up = jnp.dot(x, up_weight[...], preferred_element_type=f32)
    active = (gate * (1.0 / (1.0 + jnp.exp(-gate))) * up).astype(bf16)
    y = jnp.dot(active, down_weight[...], preferred_element_type=f32)
    for k in range(8):
        rows[:, k, :] = y[:, k * LANES : (k + 1) * LANES]
    out[...] = rows[...].astype(bf16)


def row_kernel(recv, hidden, out):
    total = hidden[...]
    for s in range(recv.shape[0]):
        total = total + recv[s].astype(f32)
    row = total.astype(bf16)
    for s in range(16):
        out[s] = row


def leave_kernel(slots, dests, recv, out):
    shape = (8, LANES)
    code = jnp.where(row_ids(shape) == 0, dests[0, 0], dests[0, 1]).astype(f32).astype(bf16)
    for s in range(out.shape[0]):
        out[s, 0:8, :] = recv[slots[0, 0]]
        out[s, 8:16, :] = recv[slots[0, 1]]
        out[s, 16:24, :] = code


def finish_kernel(
    pages, slots, rows_all, recv, pool, gathered, memory,
    rows_out, pool_out, memory_out,
    codes, rows, raw, wide, pool_sem, page_sem, raw_sem, wide_sem,
):
    t = lax.axis_index("tp")
    me = lax.axis_index("rep")
    half = t // 8
    sources = recv.shape[0]
    codes[...] = recv[:, 16:24, :].astype(f32)
    shape = (sources, LANES)
    row = row_ids(shape)
    base = [
        pltpu.make_async_copy(pool.at[p], pool_out.at[p], pool_sem.at[p])
        for p in range(pool.shape[0])
    ]
    taken = [pages[2 * slots[0, m] + half] for m in range(2)]
    for p, copy in enumerate(base):

        @pl.when((taken[0] != p) & (taken[1] != p))
        def _(copy=copy):
            copy.start()

    moved = []
    for m in range(2):
        match = codes[:, m, :] == me.astype(f32)
        source = jnp.max(jnp.where(match, row, 0))
        page_in = pltpu.make_async_copy(
            gathered.at[source, pl.ds(m * LANES, LANES), :], pool_out.at[taken[m]], page_sem.at[m]
        )
        raw_in = pltpu.make_async_copy(
            gathered.at[source, pl.ds(2 * LANES, 64), :], raw.at[m], raw_sem.at[m]
        )
        page_in.start()
        raw_in.start()
        moved.append((page_in, raw_in, source))
    rows[...] = rows_all[...].astype(f32)
    for m in range(2):
        rows[slots[0, m]] = recv[moved[m][2], 8 * m : 8 * m + 8, :].astype(f32)
    for k in range(8):
        rows_out[:, k * LANES : (k + 1) * LANES] = rows[:, k, :].astype(bf16)
    for m in range(2):
        moved[m][1].wait()
        wide[m] = raw[m, :, m * LANES : (m + 1) * LANES].astype(f32)
        pltpu.make_async_copy(wide.at[m], memory_out.at[slots[0, m]], wide_sem.at[m]).start()
    for m in range(2):
        pltpu.make_async_copy(wide.at[m], memory_out.at[slots[0, m]], wide_sem.at[m]).wait()
        moved[m][0].wait()
    for p, copy in enumerate(base):

        @pl.when((taken[0] != p) & (taken[1] != p))
        def _(copy=copy):
            copy.wait()


def body(
    tokens,
    lengths,
    prompt_group,
    span_close,
    out_slot,
    move_dest,
    page_table,
    cache_pool,
    prefix_cache,
    memory,
    norm_attn,
    norm_mlp,
    qkv_weight,
    out_weight,
    gate_weight,
    up_weight,
    down_weight,
    forget,
    write_rate,
):
    shape = jax.ShapeDtypeStruct
    rows = tokens.shape[0]
    n_tp = lax.axis_size("tp")
    n_rep = lax.axis_size("rep")
    pages = page_table.reshape(-1)
    pool = cache_pool[:, 0]
    prefix = prefix_cache[:, 0]
    mem = memory[:, 0]
    pair_weight = lax.ppermute(
        out_weight, "tp", [(i, (i + n_tp // 2) % n_tp) for i in range(n_tp)]
    )

    qkv_slots = call(
        qkv_kernel, shape((n_tp, rows, LANES), bf16), [VMEM] * 3
    )(tokens, norm_attn.reshape(1, -1), qkv_weight)
    qkv_recv = lax.all_to_all(qkv_slots, "tp", 0, 0)

    terms, mem_after, send = call(
        attend_kernel,
        (
            shape((n_tp, 24, LANES), bf16),
            shape(mem.shape, f32),
            shape((2 * LANES + 64, 2 * LANES), bf16),
        ),
        [SMEM] * 7 + [VMEM] * 6,
        scratch=[pltpu.VMEM((rows, rows * 64), f32), pltpu.VMEM((rows, 24, LANES), f32)],
    )(
        lengths, prompt_group, span_close, pages, out_slot, forget, write_rate,
        qkv_recv, pool, prefix, mem, out_weight, pair_weight,
    )
    gathered = lax.all_gather(send, "rep", axis=0)
    terms_recv = lax.all_to_all(terms, "tp", 0, 0)

    hidden, normed_slots = call(
        hidden_kernel,
        (shape((8, LANES), f32), shape((n_tp, 8, LANES), bf16)),
        [VMEM] * 3,
        scratch=[pltpu.VMEM((n_tp, 24, LANES), f32)],
    )(terms_recv, tokens, norm_mlp.reshape(8, LANES))
    normed_recv = lax.all_to_all(normed_slots, "tp", 0, 0)

    down_slots = call(
        mlp_kernel,
        shape((n_tp, 8, LANES), bf16),
        [VMEM] * 4,
        scratch=[pltpu.VMEM((rows, 8, LANES), f32)],
    )(normed_recv, gate_weight, up_weight, down_weight)
    down_recv = lax.all_to_all(down_slots, "tp", 0, 0)

    row_slots = call(row_kernel, shape((n_tp, 8, LANES), bf16), [VMEM] * 2)(down_recv, hidden)
    rows_all = lax.all_to_all(row_slots, "tp", 0, 0)

    leaving = call(
        leave_kernel, shape((n_rep, 24, LANES), bf16), [SMEM, SMEM, VMEM]
    )(out_slot, move_dest, rows_all)
    arrived = lax.all_to_all(leaving, "rep", 0, 0)

    rows_out, pool_out, mem_out = call(
        finish_kernel,
        (shape(tokens.shape, bf16), shape(pool.shape, bf16), shape(mem.shape, f32)),
        [SMEM, SMEM, VMEM, VMEM, HBM, HBM, HBM],
        out_specs=(VMEM, HBM, HBM),
        scratch=[
            pltpu.VMEM((n_rep, 8, LANES), f32),
            pltpu.VMEM((rows, 8, LANES), f32),
            pltpu.VMEM((2, 64, 2 * LANES), bf16),
            pltpu.VMEM((2, 64, LANES), f32),
            pltpu.SemaphoreType.DMA((pool.shape[0],)),
            pltpu.SemaphoreType.DMA((2,)),
            pltpu.SemaphoreType.DMA((2,)),
            pltpu.SemaphoreType.DMA((2,)),
        ],
        aliases={6: 2},
    )(pages, out_slot, rows_all, arrived, pool, gathered, mem_after)
    return rows_out, mem_out[:, None], pool_out[:, None]


def solution(mesh):
    placed = (
        P("rep", None),
        P("rep"),
        P("rep"),
        P("rep"),
        P("rep", None),
        P("rep", None),
        P("rep", None, None),
        P("rep", "tp", None, None),
        P(None, "tp", None, None),
        P("rep", "tp", None, None),
        P(),
        P(),
        P(None, "tp"),
        P("tp", None),
        P(None, "tp"),
        P(None, "tp"),
        P("tp", None),
        P(),
        P(),
    )
    return jax.shard_map(
        body,
        mesh=mesh,
        in_specs=placed,
        out_specs=(P("rep", None), P("rep", "tp", None, None), P("rep", "tp", None, None)),
        check_vma=False,
    )
```

```python
import jax
import jax.numpy as jnp
from jax import lax
from jax.experimental import pallas as pl
from jax.experimental.pallas import tpu as pltpu
from jax.sharding import PartitionSpec as P

f32 = jnp.float32
bf16 = jnp.bfloat16
highest = lax.Precision.HIGHEST
LANES = 128
NT = (((1,), (1,)), ((), ()))

VMEM = pl.BlockSpec(memory_space=pltpu.VMEM)
SMEM = pl.BlockSpec(memory_space=pltpu.SMEM)
HBM = pl.BlockSpec(memory_space=pltpu.MemorySpace.HBM)


def call(kernel, outs, in_specs, out_specs=None, scratch=(), aliases=None):
    return pl.pallas_call(
        kernel,
        out_shape=outs,
        in_specs=in_specs,
        out_specs=out_specs if out_specs is not None else jax.tree.map(lambda _: VMEM, outs),
        scratch_shapes=scratch,
        input_output_aliases=aliases or {},
        compiler_params=pltpu.CompilerParams(vmem_limit_bytes=24 << 20),
    )


def in_hbm(*arrays):
    return [pltpu.with_memory_space_constraint(a, pltpu.MemorySpace.HBM) for a in arrays]


def lane_ids(shape):
    return lax.broadcasted_iota(jnp.int32, shape, len(shape) - 1)


def row_ids(shape):
    return lax.broadcasted_iota(jnp.int32, shape, len(shape) - 2)


def column(read, count):
    rows = row_ids((count, LANES))
    out = jnp.zeros((count, LANES), jnp.int32)
    for r in range(count):
        out = jnp.where(rows == r, read(r), out)
    return out


def half_swap(block):
    return pltpu.roll(block, LANES // 2, 1)


def qkv_kernel(
    tokens_hbm, gain_hbm, weight_hbm, mlp_gain_hbm, out, kept, tokens, gain, weight, sems
):
    loads = [
        pltpu.make_async_copy(tokens_hbm, tokens, sems.at[0]),
        pltpu.make_async_copy(gain_hbm, gain, sems.at[1]),
        pltpu.make_async_copy(weight_hbm, weight, sems.at[2]),
        pltpu.make_async_copy(mlp_gain_hbm, kept.at[1], sems.at[3]),
    ]
    for load in loads:
        load.start()
    t = lax.axis_index("tp")
    loads[0].wait()
    loads[1].wait()
    x = tokens[...].astype(f32)
    row = jnp.sum(jnp.where(row_ids(x.shape) == t, x, 0.0), axis=0, keepdims=True)
    kept[0] = jnp.concatenate([row[:, k * LANES : (k + 1) * LANES] for k in range(8)], axis=0)
    scale = lax.rsqrt(jnp.mean(x * x, axis=-1, keepdims=True) + 1e-05)
    normed = (x * scale * gain[...]).astype(bf16)
    loads[2].wait()
    part = lax.dot_general(normed, weight[...], NT, preferred_element_type=f32)
    part = part.astype(bf16).astype(f32)
    first = part[:, :LANES]
    last = part[:, LANES:]
    turned = half_swap(first)
    lanes = lane_ids(first.shape)
    low = lanes < 64
    blocks = (
        jnp.where(low, first, turned),
        jnp.where(low, turned, first),
        jnp.concatenate([last, last], axis=1),
    )
    placed = []
    for j, block in enumerate(blocks):
        sub = lax.rem(3 * t + j, 2)
        placed.append(jnp.where(lanes // 64 == sub, block, 0.0))
    for head in range(8):
        slot = jnp.zeros(first.shape, f32)
        for j in range(3):
            mine = lax.rem(3 * t + j, 16) // 2 == head
            slot = slot + jnp.where(mine, placed[j], 0.0)
        out[head] = slot.astype(bf16)
        out[head + 8] = slot.astype(bf16)
    loads[3].wait()


def load_kernel(
    lengths_hbm, groups_hbm, span_hbm, pages_hbm, slots_hbm, forget_hbm, rate_hbm,
    pool_hbm, prefix_hbm,
    columns, marks, rates, pool, prefix,
    lengths, groups, span, pages, slots, forget, rate, small_sems, sems,
):
    small = [
        pltpu.make_async_copy(src, dst, small_sems.at[i])
        for i, (src, dst) in enumerate((
            (lengths_hbm, lengths), (groups_hbm, groups), (span_hbm, span), (pages_hbm, pages),
            (slots_hbm, slots), (forget_hbm, forget), (rate_hbm, rate),
        ))
    ]
    big = [
        pltpu.make_async_copy(pool_hbm, pool, sems.at[0]),
        pltpu.make_async_copy(prefix_hbm, prefix, sems.at[1]),
    ]
    for load in small + big:
        load.start()
    t = lax.axis_index("tp")
    half = t // 8
    head = lax.rem(t, 8)
    rows = columns.shape[1]
    for load in small:
        load.wait()
    columns[0] = column(lambda r: lengths[r], rows)
    columns[1] = column(lambda r: groups[r], rows)
    columns[2] = column(lambda r: pages[half, r], rows)
    columns[3] = column(lambda r: span[r], rows)
    mark_row = row_ids(marks.shape)
    marks[...] = jnp.where(mark_row == 0, slots[0, 0], slots[0, 1])
    rates[...] = jnp.where(mark_row == 0, forget[head], rate[head])
    for load in big:
        load.wait()


def pick(recv, kind, head):
    one = (16 * kind + 2 * head) // 3
    two = (16 * kind + 2 * head + 1) // 3
    a = recv[one].astype(f32)
    b = recv[two].astype(f32)
    return jnp.where(one == two, a, a + b)


def attend_kernel(recv, columns, pool, prefix, away_out, here_out):
    t = lax.axis_index("tp")
    half = t // 8
    head = lax.rem(t, 8)
    query = pick(recv, 0, head)
    key = pick(recv, 1, head)
    value = pick(recv, 2, head)
    rows = query.shape[0]
    lanes = lane_ids((rows, LANES))
    low = lanes < 64
    length = columns[0]
    group = columns[1]
    page = columns[2]
    score_scale = LANES ** (-0.5)
    page_count = pool.shape[0]
    query_b = query.astype(bf16)
    pool_keys = pool[:, :, :LANES].reshape(page_count * LANES, LANES)
    pool_scores = lax.dot_general(query_b, pool_keys, NT, preferred_element_type=f32)
    pre_rows = prefix.shape[0] * prefix.shape[1]
    pre_keys = prefix[:, :, :LANES].reshape(pre_rows, LANES)
    pre_scores = lax.dot_general(query_b, pre_keys, NT, preferred_element_type=f32)
    tiles = []
    in_reach = lanes + half * LANES < length
    for p in range(page_count):
        live = (page == p) & in_reach
        tile = pool_scores[:, p * LANES : (p + 1) * LANES] * score_scale
        tiles.append(jnp.where(live, tile, -jnp.inf))
    for p in range(pre_rows // LANES):
        live = group == lanes // 64 + 2 * p
        tile = pre_scores[:, p * LANES : (p + 1) * LANES] * score_scale
        tiles.append(jnp.where(live, tile, -jnp.inf))
    own = jnp.sum(query * key, axis=-1, keepdims=True) * score_scale
    own = jnp.where(half == 0, own, -jnp.inf)
    peak = tiles[0]
    for tile in tiles[1:]:
        peak = jnp.maximum(peak, tile)
    top = jnp.maximum(jnp.max(peak, axis=-1, keepdims=True), own)
    weights = [jnp.exp(tile - top) for tile in tiles]
    own_weight = jnp.exp(own - top)
    total = weights[0]
    for tile in weights[1:]:
        total = total + tile
    denom = jnp.sum(total, axis=-1, keepdims=True) + own_weight

    def both(parts):
        full = jnp.concatenate(parts, axis=1)
        upper = full.astype(bf16)
        lower = (full - upper.astype(f32)).astype(bf16)
        return jnp.concatenate([upper, lower], axis=0)

    pool_values = pool[:, :, LANES:].reshape(page_count * LANES, LANES)
    pre_values = prefix[:, :, LANES:].reshape(pre_rows, LANES)
    summed = jnp.dot(both(weights[:page_count]), pool_values, preferred_element_type=f32)
    summed = summed + jnp.dot(
        both(weights[page_count:]), pre_values, preferred_element_type=f32
    )
    summed = summed[:rows] + summed[rows:] + own_weight * value
    attended = summed / denom
    lse = top + jnp.log(denom)
    swapped = half_swap(attended)
    here_out[...] = jnp.where(low, jnp.where(half == 0, attended, swapped), lse)
    away_out[...] = jnp.where(low, jnp.where(half == 0, swapped, attended), lse)


def memory_kernel(
    slots_hbm, dests_hbm, pages_hbm, memory_hbm, weight_hbm, gate_hbm, up_hbm, down_hbm,
    recv, columns, rates, pool, here,
    memory_out, recalled_out, send_out, pool_out, weight, gate, up, down,
    slots, dests, pages, memory, masked, small_sems, sems, out_sem,
):
    del here
    small = [
        pltpu.make_async_copy(slots_hbm, slots, small_sems.at[0]),
        pltpu.make_async_copy(dests_hbm, dests, small_sems.at[1]),
        pltpu.make_async_copy(pages_hbm, pages, small_sems.at[2]),
    ]
    big = [
        pltpu.make_async_copy(src, dst, sems.at[i])
        for i, (src, dst) in enumerate((
            (memory_hbm, memory), (weight_hbm, weight), (gate_hbm, gate), (up_hbm, up),
            (down_hbm, down),
        ))
    ]
    pool_copy = pltpu.make_async_copy(pool, pool_out, out_sem)
    for load in small + big + [pool_copy]:
        load.start()
    t = lax.axis_index("tp")
    half = t // 8
    head = lax.rem(t, 8)
    query = pick(recv, 0, head)
    key = pick(recv, 1, head)
    value = pick(recv, 2, head)
    rows = query.shape[0]
    shape = query.shape
    lanes = lane_ids(shape)
    row = row_ids(shape)
    low = lanes < 64
    query_unit = query * lax.rsqrt(jnp.sum(query * query, axis=-1, keepdims=True) + 1e-06)
    key_unit = key * lax.rsqrt(jnp.sum(key * key, axis=-1, keepdims=True) + 1e-06)
    mem_rows = memory.shape[1]
    big[0].wait()
    flat_memory = memory[...].reshape(rows * mem_rows, LANES)
    seen = lax.dot_general(
        jnp.concatenate([query_unit, key_unit], axis=0), flat_memory, NT,
        preferred_element_type=f32, precision=highest,
    )
    recalled = jnp.zeros(shape, f32)
    value_half = jnp.where(half == 0, value, half_swap(value))
    value_both = jnp.where(low, value_half, half_swap(value_half))
    closing = columns[3] == 1
    keep = rates[0:1]
    step = rates[1:2]
    for c in range(rows // 2):
        mine = row == 2 * c + lanes // 64
        cut = slice(c * LANES, (c + 1) * LANES)
        recalled = recalled + jnp.where(mine, seen[:rows, cut], 0.0)
        misfit = (value_both - seen[rows:, cut]) * step
        masked[:, cut] = jnp.where(mine & closing, misfit, 0.0)
    recalled_out[...] = recalled + half_swap(recalled)
    change = lax.dot_general(
        masked[...], key_unit, (((0,), (0,)), ((), ())),
        preferred_element_type=f32, precision=highest,
    )
    decay = jnp.where(closing, keep, 1.0)
    for r in range(rows):
        memory_out[r] = decay[r : r + 1] * memory[r] + change[r * mem_rows : (r + 1) * mem_rows]
    for load in small:
        load.wait()
    for m in range(2):
        slot = slots[0, m]
        send_out[m * LANES : (m + 1) * LANES, :] = pool[pages[half, slot]]
        send_out[2 * LANES : 2 * LANES + 64, m * LANES : (m + 1) * LANES] = memory_out[
            slot
        ].astype(bf16)
    code = jnp.where(row_ids((8, 2 * LANES)) == 0, dests[0, 0], dests[0, 1])
    send_out[2 * LANES + 64 :, :] = code.astype(f32).astype(bf16)
    for load in big[1:] + [pool_copy]:
        load.wait()


def spread(rows, wide):
    for k in range(8):
        rows[:, k, :] = wide[:, k * LANES : (k + 1) * LANES]


def project_kernel(here, away, recalled, weight, out, rows):
    mine = here[...]
    other = away[...]
    lse = mine[:, 64:65]
    lse_other = other[:, 64:65]
    share = 1.0 / (1.0 + jnp.exp(lse_other - lse))
    share_other = 1.0 / (1.0 + jnp.exp(lse - lse_other))
    mixed = share * mine + share_other * other + recalled[...]
    mixed = mixed.astype(bf16)[:, :64]
    spread(rows, jnp.dot(mixed, weight[...], preferred_element_type=f32))
    out[...] = rows[...].astype(bf16)


def hidden_kernel(recv, kept, hidden_out, normed_out):
    hidden = kept[0]
    for s in range(recv.shape[0]):
        hidden = hidden + recv[s].astype(f32)
    hidden_out[...] = hidden
    square = jnp.sum(jnp.sum(hidden * hidden, axis=1, keepdims=True), axis=0, keepdims=True)
    scale = lax.rsqrt(square / (8 * LANES) + 1e-05)
    normed = (hidden * scale * kept[1]).astype(bf16)
    for s in range(normed_out.shape[0]):
        normed_out[s] = normed


def mlp_kernel(recv, gate_weight, up_weight, down_weight, out, rows):
    rows[...] = recv[...].astype(f32)
    x = jnp.concatenate([rows[:, k, :] for k in range(8)], axis=1).astype(bf16)
    gate = lax.dot_general(x, gate_weight[...], NT, preferred_element_type=f32)
    up = lax.dot_general(x, up_weight[...], NT, preferred_element_type=f32)
    active = (gate * (1.0 / (1.0 + jnp.exp(-gate))) * up).astype(bf16)
    spread(rows, jnp.dot(active, down_weight[...], preferred_element_type=f32))
    out[...] = rows[...].astype(bf16)


def row_kernel(recv, hidden, out):
    total = hidden[...]
    for s in range(recv.shape[0]):
        total = total + recv[s].astype(f32)
    row = total.astype(bf16)
    for s in range(16):
        out[s] = row


def leave_kernel(marks, recv, out):
    leaving = []
    for m in range(2):
        mark = marks[m : m + 1]
        row = jnp.zeros(recv.shape[1:], f32)
        for s in range(recv.shape[0]):
            row = jnp.where(mark == s, recv[s].astype(f32), row)
        leaving.append(row)
    both = jnp.concatenate(leaving, axis=0).astype(bf16)
    for s in range(out.shape[0]):
        out[s] = both


def place_kernel(
    pages_hbm, slots_hbm, pool, memory, gathered, pool_out, memory_out, codes_out,
    pages, slots, codes, page, raw, wide, small_sems, page_sem, raw_sem, wide_sem,
):
    small = [
        pltpu.make_async_copy(pages_hbm, pages, small_sems.at[0]),
        pltpu.make_async_copy(slots_hbm, slots, small_sems.at[1]),
        pltpu.make_async_copy(
            gathered.at[:, pl.ds(2 * LANES + 64, 8), pl.ds(0, LANES)], codes, small_sems.at[2]
        ),
    ]
    for load in small:
        load.start()
    half = lax.axis_index("tp") // 8
    me = lax.axis_index("rep").astype(f32)
    for load in small:
        load.wait()
    all_codes = codes[...].astype(f32)
    codes_out[...] = all_codes
    row = row_ids((codes.shape[0], LANES))
    moved = []
    for m in range(2):
        source = jnp.max(jnp.where(codes_out[:, m, :] == me, row, 0))
        page_in = pltpu.make_async_copy(
            gathered.at[source, pl.ds(m * LANES, LANES), :], page.at[m], page_sem.at[m]
        )
        raw_in = pltpu.make_async_copy(
            gathered.at[source, pl.ds(2 * LANES, 64), pl.ds(m * LANES, LANES)],
            raw.at[m],
            raw_sem.at[m],
        )
        page_in.start()
        raw_in.start()
        moved.append((page_in, raw_in))
    stores = []
    for m in range(2):
        moved[m][0].wait()
        place = pool_out.at[pages[half, slots[0, m]]]
        stores.append(pltpu.make_async_copy(page.at[m], place, page_sem.at[2 + m]))
        stores[-1].start()
    for m in range(2):
        moved[m][1].wait()
        wide[m] = raw[m].astype(f32)
        place = memory_out.at[slots[0, m]]
        stores.append(pltpu.make_async_copy(wide.at[m], place, wide_sem.at[m]))
        stores[-1].start()
    for store in stores:
        store.wait()


def rows_kernel(marks, rows_all, recv, codes, rows_out, rows):
    me = lax.axis_index("rep").astype(f32)
    arriving = []
    for m in range(2):
        row = jnp.zeros(rows_all.shape[1:], f32)
        for s in range(recv.shape[0]):
            part = recv[s, 8 * m : 8 * m + 8, :].astype(f32)
            row = jnp.where(codes[s, m : m + 1, :] == me, part, row)
        arriving.append(row)
    for s in range(rows_all.shape[0]):
        row = rows_all[s].astype(f32)
        for m in range(2):
            row = jnp.where(marks[m : m + 1] == s, arriving[m], row)
        rows[s] = row
    for k in range(8):
        rows_out[:, k * LANES : (k + 1) * LANES] = rows[:, k, :].astype(bf16)


def body(
    tokens,
    lengths,
    prompt_group,
    span_close,
    out_slot,
    move_dest,
    page_table,
    cache_pool,
    prefix_cache,
    memory,
    norm_attn,
    norm_mlp,
    qkv_weight,
    out_weight,
    gate_weight,
    up_weight,
    down_weight,
    forget,
    write_rate,
):
    shape = jax.ShapeDtypeStruct
    rows = tokens.shape[0]
    n_tp = lax.axis_size("tp")
    n_rep = lax.axis_size("rep")
    pages = page_table.transpose(2, 1, 0)[0]
    pool = cache_pool[:, 0]
    prefix = prefix_cache[:, 0]
    mem = memory[:, 0]
    send_shape = shape((2 * LANES + 72, 2 * LANES), bf16)

    qkv_slots, kept = call(
        qkv_kernel,
        (shape((n_tp, rows, LANES), bf16), shape((2, 8, LANES), f32)),
        [HBM] * 4,
        scratch=[
            pltpu.VMEM(tokens.shape, bf16),
            pltpu.VMEM((1, tokens.shape[1]), f32),
            pltpu.VMEM(qkv_weight.shape[::-1], bf16),
            pltpu.SemaphoreType.DMA((4,)),
        ],
    )(*in_hbm(tokens, norm_attn.reshape(1, -1), qkv_weight.T, norm_mlp.reshape(8, LANES)))
    qkv_recv = lax.all_to_all(qkv_slots, "tp", 0, 0)

    gate = gate_weight.T
    up = up_weight.T
    columns, marks, rates, pool_near, prefix_near = call(
        load_kernel,
        (
            shape((4, rows, LANES), jnp.int32),
            shape((8, LANES), jnp.int32),
            shape((8, LANES), f32),
            shape(pool.shape, bf16),
            shape(prefix.shape, bf16),
        ),
        [HBM] * 9,
        scratch=[
            pltpu.SMEM((rows,), jnp.int32),
            pltpu.SMEM((rows,), jnp.int32),
            pltpu.SMEM((rows,), jnp.int32),
            pltpu.SMEM(pages.shape, jnp.int32),
            pltpu.SMEM(out_slot.shape, jnp.int32),
            pltpu.SMEM(forget.shape, f32),
            pltpu.SMEM(write_rate.shape, f32),
            pltpu.SemaphoreType.DMA((7,)),
            pltpu.SemaphoreType.DMA((2,)),
        ],
    )(
        *in_hbm(lengths, prompt_group, span_close, pages, out_slot, forget, write_rate),
        *in_hbm(pool, prefix),
    )

    away, here = call(
        attend_kernel, (shape((rows, LANES), f32), shape((rows, LANES), f32)), [VMEM] * 4
    )(qkv_recv, columns, pool_near, prefix_near)
    away_recv = lax.ppermute(away, "tp", [(i, (i + n_tp // 2) % n_tp) for i in range(n_tp)])
    mem_after, recalled, send, pool_base, out_near, gate_near, up_near, down_near = call(
        memory_kernel,
        (
            shape(mem.shape, f32),
            shape((rows, LANES), f32),
            send_shape,
            shape(pool.shape, bf16),
            shape(out_weight.shape, bf16),
            shape(gate.shape, bf16),
            shape(up.shape, bf16),
            shape(down_weight.shape, bf16),
        ),
        [HBM] * 8 + [VMEM] * 4 + [HBM],
        out_specs=(VMEM,) * 3 + (HBM,) + (VMEM,) * 4,
        scratch=[
            pltpu.SMEM(out_slot.shape, jnp.int32),
            pltpu.SMEM(move_dest.shape, jnp.int32),
            pltpu.SMEM(pages.shape, jnp.int32),
            pltpu.VMEM(mem.shape, f32),
            pltpu.VMEM((rows, rows * 64), f32),
            pltpu.SemaphoreType.DMA((3,)),
            pltpu.SemaphoreType.DMA((5,)),
            pltpu.SemaphoreType.DMA,
        ],
    )(
        *in_hbm(out_slot, move_dest, pages, mem, out_weight, gate, up, down_weight),
        qkv_recv, columns, rates, pool_near, here,
    )
    gathered = lax.all_gather(send, "rep", axis=0)

    row_scratch = pltpu.VMEM((rows, 8, LANES), f32)
    terms = call(
        project_kernel, shape((n_tp, 8, LANES), bf16), [VMEM] * 4, scratch=[row_scratch]
    )(here, away_recv, recalled, out_near)
    terms_recv = lax.all_to_all(terms, "tp", 0, 0)

    hidden, normed_slots = call(
        hidden_kernel,
        (shape((8, LANES), f32), shape((n_tp, 8, LANES), bf16)),
        [VMEM] * 2,
    )(terms_recv, kept)
    normed_recv = lax.all_to_all(normed_slots, "tp", 0, 0)

    down_slots = call(
        mlp_kernel, shape((n_tp, 8, LANES), bf16), [VMEM] * 4, scratch=[row_scratch]
    )(normed_recv, gate_near, up_near, down_near)
    down_recv = lax.all_to_all(down_slots, "tp", 0, 0)

    row_slots = call(row_kernel, shape((n_tp, 8, LANES), bf16), [VMEM] * 2)(down_recv, hidden)
    rows_all = lax.all_to_all(row_slots, "tp", 0, 0)

    leaving = call(leave_kernel, shape((n_rep, 16, LANES), bf16), [VMEM] * 2)(marks, rows_all)
    arrived = lax.all_to_all(leaving, "rep", 0, 0)

    pool_out, mem_out, codes = call(
        place_kernel,
        (shape(pool.shape, bf16), shape(mem.shape, f32), shape((n_rep, 8, LANES), f32)),
        [HBM] * 5,
        out_specs=(HBM, HBM, VMEM),
        scratch=[
            pltpu.SMEM(pages.shape, jnp.int32),
            pltpu.SMEM(out_slot.shape, jnp.int32),
            pltpu.VMEM((n_rep, 8, LANES), bf16),
            pltpu.VMEM((2, LANES, 2 * LANES), bf16),
            pltpu.VMEM((2, 64, LANES), bf16),
            pltpu.VMEM((2, 64, LANES), f32),
            pltpu.SemaphoreType.DMA((3,)),
            pltpu.SemaphoreType.DMA((4,)),
            pltpu.SemaphoreType.DMA((2,)),
            pltpu.SemaphoreType.DMA((2,)),
        ],
        aliases={2: 0, 3: 1},
    )(*in_hbm(pages, out_slot, pool_base, mem_after, gathered))
    rows_out = call(
        rows_kernel, shape(tokens.shape, bf16), [VMEM] * 4, scratch=[row_scratch]
    )(marks, rows_all, arrived, codes)
    return rows_out, mem_out[:, None], pool_out[:, None]


def solution(mesh):
    placed = (
        P("rep", None),
        P("rep"),
        P("rep"),
        P("rep"),
        P("rep", None),
        P("rep", None),
        P("rep", None, None),
        P("rep", "tp", None, None),
        P(None, "tp", None, None),
        P("rep", "tp", None, None),
        P(),
        P(),
        P(None, "tp"),
        P("tp", None),
        P(None, "tp"),
        P(None, "tp"),
        P("tp", None),
        P(),
        P(),
    )
    return jax.shard_map(
        body,
        mesh=mesh,
        in_specs=placed,
        out_specs=(P("rep", None), P("rep", "tp", None, None), P("rep", "tp", None, None)),
        check_vma=False,
    )
```

```python
import jax
import jax.numpy as jnp
from jax import lax
from jax.experimental import pallas as pl
from jax.experimental.pallas import tpu as pltpu
from jax.sharding import PartitionSpec as P

f32 = jnp.float32
bf16 = jnp.bfloat16
highest = lax.Precision.HIGHEST
LANES = 128
NT = (((1,), (1,)), ((), ()))

VMEM = pl.BlockSpec(memory_space=pltpu.VMEM)
SMEM = pl.BlockSpec(memory_space=pltpu.SMEM)
HBM = pl.BlockSpec(memory_space=pltpu.MemorySpace.HBM)


def call(kernel, outs, in_specs, out_specs=None, scratch=(), aliases=None):
    return pl.pallas_call(
        kernel,
        out_shape=outs,
        in_specs=in_specs,
        out_specs=out_specs if out_specs is not None else jax.tree.map(lambda _: VMEM, outs),
        scratch_shapes=scratch,
        input_output_aliases=aliases or {},
        compiler_params=pltpu.CompilerParams(vmem_limit_bytes=24 << 20),
    )


def in_hbm(*arrays):
    return [pltpu.with_memory_space_constraint(a, pltpu.MemorySpace.HBM) for a in arrays]


def lane_ids(shape):
    return lax.broadcasted_iota(jnp.int32, shape, len(shape) - 1)


def row_ids(shape):
    return lax.broadcasted_iota(jnp.int32, shape, len(shape) - 2)


def column(read, count):
    rows = row_ids((count, LANES))
    out = jnp.zeros((count, LANES), jnp.int32)
    for r in range(count):
        out = jnp.where(rows == r, read(r), out)
    return out


def half_swap(block):
    return pltpu.roll(block, LANES // 2, 1)


def qkv_kernel(
    tokens_hbm, gain_hbm, weight_hbm, mlp_gain_hbm, out, kept, tokens, gain, weight, sems
):
    loads = [
        pltpu.make_async_copy(tokens_hbm, tokens, sems.at[0]),
        pltpu.make_async_copy(gain_hbm, gain, sems.at[1]),
        pltpu.make_async_copy(weight_hbm, weight, sems.at[2]),
        pltpu.make_async_copy(mlp_gain_hbm, kept.at[1], sems.at[3]),
    ]
    for load in loads:
        load.start()
    t = lax.axis_index("tp")
    loads[0].wait()
    loads[1].wait()
    x = tokens[...].astype(f32)
    row = jnp.sum(jnp.where(row_ids(x.shape) == t, x, 0.0), axis=0, keepdims=True)
    kept[0] = jnp.concatenate([row[:, k * LANES : (k + 1) * LANES] for k in range(8)], axis=0)
    scale = lax.rsqrt(jnp.mean(x * x, axis=-1, keepdims=True) + 1e-05)
    normed = (x * scale * gain[...]).astype(bf16)
    loads[2].wait()
    part = lax.dot_general(normed, weight[...], NT, preferred_element_type=f32)
    part = part.astype(bf16).astype(f32)
    first = part[:, :LANES]
    last = part[:, LANES:]
    turned = half_swap(first)
    lanes = lane_ids(first.shape)
    low = lanes < 64
    blocks = (
        jnp.where(low, first, turned),
        jnp.where(low, turned, first),
        jnp.concatenate([last, last], axis=1),
    )
    placed = []
    for j, block in enumerate(blocks):
        sub = lax.rem(3 * t + j, 2)
        placed.append(jnp.where(lanes // 64 == sub, block, 0.0))
    for head in range(8):
        slot = jnp.zeros(first.shape, f32)
        for j in range(3):
            mine = lax.rem(3 * t + j, 16) // 2 == head
            slot = slot + jnp.where(mine, placed[j], 0.0)
        out[head] = slot.astype(bf16)
        out[head + 8] = slot.astype(bf16)
    loads[3].wait()


def load_kernel(
    lengths_hbm, groups_hbm, span_hbm, pages_hbm, slots_hbm, forget_hbm, rate_hbm,
    pool_hbm, prefix_hbm, memory_hbm, weight_hbm, gate_hbm, up_hbm, down_hbm,
    columns, marks, rates, pool, prefix, memory, weight, gate, up, down,
    lengths, groups, span, pages, slots, forget, rate, small_sems, sems,
):
    small = [
        pltpu.make_async_copy(src, dst, small_sems.at[i])
        for i, (src, dst) in enumerate((
            (lengths_hbm, lengths), (groups_hbm, groups), (span_hbm, span), (pages_hbm, pages),
            (slots_hbm, slots), (forget_hbm, forget), (rate_hbm, rate),
        ))
    ]
    big = [
        pltpu.make_async_copy(src, dst, sems.at[i])
        for i, (src, dst) in enumerate((
            (pool_hbm, pool), (prefix_hbm, prefix), (memory_hbm, memory), (weight_hbm, weight),
            (gate_hbm, gate), (up_hbm, up), (down_hbm, down),
        ))
    ]
    for load in small + big:
        load.start()
    t = lax.axis_index("tp")
    half = t // 8
    head = lax.rem(t, 8)
    rows = columns.shape[1]
    for load in small:
        load.wait()
    columns[0] = column(lambda r: lengths[r], rows)
    columns[1] = column(lambda r: groups[r], rows)
    columns[2] = column(lambda r: pages[half, r], rows)
    columns[3] = column(lambda r: span[r], rows)
    mark_row = row_ids(marks.shape)
    marks[...] = jnp.where(mark_row == 0, slots[0, 0], slots[0, 1])
    rates[...] = jnp.where(mark_row == 0, forget[head], rate[head])
    for load in big:
        load.wait()


def pick(recv, kind, head):
    one = (16 * kind + 2 * head) // 3
    two = (16 * kind + 2 * head + 1) // 3
    a = recv[one].astype(f32)
    b = recv[two].astype(f32)
    return jnp.where(one == two, a, a + b)


def attend_kernel(
    slots_hbm, dests_hbm, pages_hbm, recv, columns, rates, pool, prefix, memory,
    away_out, here_out, send_out,
    slots, dests, pages, small_sems,
):
    small = [
        pltpu.make_async_copy(slots_hbm, slots, small_sems.at[0]),
        pltpu.make_async_copy(dests_hbm, dests, small_sems.at[1]),
        pltpu.make_async_copy(pages_hbm, pages, small_sems.at[2]),
    ]
    for load in small:
        load.start()
    t = lax.axis_index("tp")
    half = t // 8
    head = lax.rem(t, 8)
    query = pick(recv, 0, head)
    key = pick(recv, 1, head)
    value = pick(recv, 2, head)
    rows = query.shape[0]
    lanes = lane_ids((rows, LANES))
    low = lanes < 64
    length = columns[0]
    group = columns[1]
    page = columns[2]
    score_scale = LANES ** (-0.5)
    page_count = pool.shape[0]
    query_b = query.astype(bf16)
    pool_keys = pool[:, :, :LANES].reshape(page_count * LANES, LANES)
    pool_scores = lax.dot_general(query_b, pool_keys, NT, preferred_element_type=f32)
    pre_rows = prefix.shape[0] * prefix.shape[1]
    pre_keys = prefix[:, :, :LANES].reshape(pre_rows, LANES)
    pre_scores = lax.dot_general(query_b, pre_keys, NT, preferred_element_type=f32)
    tiles = []
    in_reach = lanes + half * LANES < length
    for p in range(page_count):
        live = (page == p) & in_reach
        tile = pool_scores[:, p * LANES : (p + 1) * LANES] * score_scale
        tiles.append(jnp.where(live, tile, -jnp.inf))
    for p in range(pre_rows // LANES):
        live = group == lanes // 64 + 2 * p
        tile = pre_scores[:, p * LANES : (p + 1) * LANES] * score_scale
        tiles.append(jnp.where(live, tile, -jnp.inf))
    own = jnp.sum(query * key, axis=-1, keepdims=True) * score_scale
    own = jnp.where(half == 0, own, -jnp.inf)
    peak = tiles[0]
    for tile in tiles[1:]:
        peak = jnp.maximum(peak, tile)
    top = jnp.maximum(jnp.max(peak, axis=-1, keepdims=True), own)
    weights = [jnp.exp(tile - top) for tile in tiles]
    own_weight = jnp.exp(own - top)
    total = weights[0]
    for tile in weights[1:]:
        total = total + tile
    denom = jnp.sum(total, axis=-1, keepdims=True) + own_weight

    def both(parts):
        full = jnp.concatenate(parts, axis=1)
        upper = full.astype(bf16)
        lower = (full - upper.astype(f32)).astype(bf16)
        return jnp.concatenate([upper, lower], axis=0)

    pool_values = pool[:, :, LANES:].reshape(page_count * LANES, LANES)
    pre_values = prefix[:, :, LANES:].reshape(pre_rows, LANES)
    summed = jnp.dot(both(weights[:page_count]), pool_values, preferred_element_type=f32)
    summed = summed + jnp.dot(
        both(weights[page_count:]), pre_values, preferred_element_type=f32
    )
    summed = summed[:rows] + summed[rows:] + own_weight * value
    attended = summed / denom
    lse = top + jnp.log(denom)
    swapped = half_swap(attended)
    here_out[...] = jnp.where(low, jnp.where(half == 0, attended, swapped), lse)
    away_out[...] = jnp.where(low, jnp.where(half == 0, swapped, attended), lse)

    key_unit = key * lax.rsqrt(jnp.sum(key * key, axis=-1, keepdims=True) + 1e-06)
    value_half = jnp.where(half == 0, value, half_swap(value))
    closing = columns[3]
    row = row_ids(lanes.shape)
    mem_shape = memory.shape[1:]
    diagonal = row_ids(mem_shape) == lane_ids(mem_shape)
    for load in small:
        load.wait()
    for m in range(2):
        slot = slots[0, m]
        mine = row == slot
        key_row = jnp.sum(jnp.where(mine, key_unit, 0.0), axis=0, keepdims=True)
        value_row = jnp.sum(jnp.where(mine, value_half, 0.0), axis=0, keepdims=True)
        closes = jnp.max(jnp.where(mine, closing, 0), axis=0, keepdims=True) == 1
        block = memory[slot]
        seen = jnp.sum(block * key_row, axis=1, keepdims=True)
        target = jnp.sum(jnp.where(diagonal, value_row, 0.0), axis=1, keepdims=True)
        written = rates[0:1] * block + rates[1:2] * (target - seen) * key_row
        written = jnp.where(closes, written, block)
        send_out[m * LANES : (m + 1) * LANES, :] = pool[pages[half, slot]]
        send_out[2 * LANES : 2 * LANES + 64, m * LANES : (m + 1) * LANES] = written.astype(bf16)
    code = jnp.where(row_ids((8, 2 * LANES)) == 0, dests[0, 0], dests[0, 1])
    send_out[2 * LANES + 64 :, :] = code.astype(f32).astype(bf16)


def memory_kernel(
    recv, columns, rates, pool, memory, memory_out, recalled_out, pool_out, masked, out_sem
):
    pool_copy = pltpu.make_async_copy(pool, pool_out, out_sem)
    pool_copy.start()
    t = lax.axis_index("tp")
    half = t // 8
    head = lax.rem(t, 8)
    query = pick(recv, 0, head)
    key = pick(recv, 1, head)
    value = pick(recv, 2, head)
    rows = query.shape[0]
    shape = query.shape
    lanes = lane_ids(shape)
    row = row_ids(shape)
    low = lanes < 64
    query_unit = query * lax.rsqrt(jnp.sum(query * query, axis=-1, keepdims=True) + 1e-06)
    key_unit = key * lax.rsqrt(jnp.sum(key * key, axis=-1, keepdims=True) + 1e-06)
    mem_rows = memory.shape[1]
    flat_memory = memory[...].reshape(rows * mem_rows, LANES)
    seen = lax.dot_general(
        jnp.concatenate([query_unit, key_unit], axis=0), flat_memory, NT,
        preferred_element_type=f32, precision=highest,
    )
    recalled = jnp.zeros(shape, f32)
    value_half = jnp.where(half == 0, value, half_swap(value))
    value_both = jnp.where(low, value_half, half_swap(value_half))
    closing = columns[3] == 1
    keep = rates[0:1]
    step = rates[1:2]
    for c in range(rows // 2):
        mine = row == 2 * c + lanes // 64
        cut = slice(c * LANES, (c + 1) * LANES)
        recalled = recalled + jnp.where(mine, seen[:rows, cut], 0.0)
        misfit = (value_both - seen[rows:, cut]) * step
        masked[:, cut] = jnp.where(mine & closing, misfit, 0.0)
    recalled_out[...] = recalled + half_swap(recalled)
    change = lax.dot_general(
        masked[...], key_unit, (((0,), (0,)), ((), ())),
        preferred_element_type=f32, precision=highest,
    )
    decay = jnp.where(closing, keep, 1.0)
    for r in range(rows):
        memory_out[r] = decay[r : r + 1] * memory[r] + change[r * mem_rows : (r + 1) * mem_rows]
    pool_copy.wait()


def spread(rows, wide):
    for k in range(8):
        rows[:, k, :] = wide[:, k * LANES : (k + 1) * LANES]


def project_kernel(here, away, recalled, weight, out, rows):
    mine = here[...]
    other = away[...]
    lse = mine[:, 64:65]
    lse_other = other[:, 64:65]
    share = 1.0 / (1.0 + jnp.exp(lse_other - lse))
    share_other = 1.0 / (1.0 + jnp.exp(lse - lse_other))
    mixed = share * mine + share_other * other + recalled[...]
    mixed = mixed.astype(bf16)[:, :64]
    spread(rows, jnp.dot(mixed, weight[...], preferred_element_type=f32))
    out[...] = rows[...].astype(bf16)


def hidden_kernel(recv, kept, hidden_out, normed_out):
    hidden = kept[0]
    for s in range(recv.shape[0]):
        hidden = hidden + recv[s].astype(f32)
    hidden_out[...] = hidden
    square = jnp.sum(jnp.sum(hidden * hidden, axis=1, keepdims=True), axis=0, keepdims=True)
    scale = lax.rsqrt(square / (8 * LANES) + 1e-05)
    normed = (hidden * scale * kept[1]).astype(bf16)
    for s in range(normed_out.shape[0]):
        normed_out[s] = normed


def mlp_kernel(recv, gate_weight, up_weight, down_weight, out, rows):
    rows[...] = recv[...].astype(f32)
    x = jnp.concatenate([rows[:, k, :] for k in range(8)], axis=1).astype(bf16)
    gate = lax.dot_general(x, gate_weight[...], NT, preferred_element_type=f32)
    up = lax.dot_general(x, up_weight[...], NT, preferred_element_type=f32)
    active = (gate * (1.0 / (1.0 + jnp.exp(-gate))) * up).astype(bf16)
    spread(rows, jnp.dot(active, down_weight[...], preferred_element_type=f32))
    out[...] = rows[...].astype(bf16)


def row_kernel(recv, hidden, out):
    total = hidden[...]
    for s in range(recv.shape[0]):
        total = total + recv[s].astype(f32)
    row = total.astype(bf16)
    for s in range(16):
        out[s] = row


def leave_kernel(marks, recv, out):
    leaving = []
    for m in range(2):
        mark = marks[m : m + 1]
        row = jnp.zeros(recv.shape[1:], f32)
        for s in range(recv.shape[0]):
            row = jnp.where(mark == s, recv[s].astype(f32), row)
        leaving.append(row)
    both = jnp.concatenate(leaving, axis=0).astype(bf16)
    for s in range(out.shape[0]):
        out[s] = both


def place_kernel(
    pages_hbm, slots_hbm, pool, memory, gathered, pool_out, memory_out, codes_out,
    pages, slots, codes, page, raw, wide, small_sems, page_sem, raw_sem, wide_sem,
):
    small = [
        pltpu.make_async_copy(pages_hbm, pages, small_sems.at[0]),
        pltpu.make_async_copy(slots_hbm, slots, small_sems.at[1]),
        pltpu.make_async_copy(
            gathered.at[:, pl.ds(2 * LANES + 64, 8), pl.ds(0, LANES)], codes, small_sems.at[2]
        ),
    ]
    for load in small:
        load.start()
    half = lax.axis_index("tp") // 8
    me = lax.axis_index("rep").astype(f32)
    for load in small:
        load.wait()
    all_codes = codes[...].astype(f32)
    codes_out[...] = all_codes
    row = row_ids((codes.shape[0], LANES))
    moved = []
    for m in range(2):
        source = jnp.max(jnp.where(codes_out[:, m, :] == me, row, 0))
        page_in = pltpu.make_async_copy(
            gathered.at[source, pl.ds(m * LANES, LANES), :], page.at[m], page_sem.at[m]
        )
        raw_in = pltpu.make_async_copy(
            gathered.at[source, pl.ds(2 * LANES, 64), pl.ds(m * LANES, LANES)],
            raw.at[m],
            raw_sem.at[m],
        )
        page_in.start()
        raw_in.start()
        moved.append((page_in, raw_in))
    stores = []
    for m in range(2):
        moved[m][0].wait()
        place = pool_out.at[pages[half, slots[0, m]]]
        stores.append(pltpu.make_async_copy(page.at[m], place, page_sem.at[2 + m]))
        stores[-1].start()
    for m in range(2):
        moved[m][1].wait()
        wide[m] = raw[m].astype(f32)
        place = memory_out.at[slots[0, m]]
        stores.append(pltpu.make_async_copy(wide.at[m], place, wide_sem.at[m]))
        stores[-1].start()
    for store in stores:
        store.wait()


def rows_kernel(marks, rows_all, recv, codes, rows_out, rows):
    me = lax.axis_index("rep").astype(f32)
    arriving = []
    for m in range(2):
        row = jnp.zeros(rows_all.shape[1:], f32)
        for s in range(recv.shape[0]):
            part = recv[s, 8 * m : 8 * m + 8, :].astype(f32)
            row = jnp.where(codes[s, m : m + 1, :] == me, part, row)
        arriving.append(row)
    for s in range(rows_all.shape[0]):
        row = rows_all[s].astype(f32)
        for m in range(2):
            row = jnp.where(marks[m : m + 1] == s, arriving[m], row)
        rows[s] = row
    for k in range(8):
        rows_out[:, k * LANES : (k + 1) * LANES] = rows[:, k, :].astype(bf16)


def body(
    tokens,
    lengths,
    prompt_group,
    span_close,
    out_slot,
    move_dest,
    page_table,
    cache_pool,
    prefix_cache,
    memory,
    norm_attn,
    norm_mlp,
    qkv_weight,
    out_weight,
    gate_weight,
    up_weight,
    down_weight,
    forget,
    write_rate,
):
    shape = jax.ShapeDtypeStruct
    rows = tokens.shape[0]
    n_tp = lax.axis_size("tp")
    n_rep = lax.axis_size("rep")
    pages = page_table.transpose(2, 1, 0)[0]
    pool = cache_pool[:, 0]
    prefix = prefix_cache[:, 0]
    mem = memory[:, 0]
    send_shape = shape((2 * LANES + 72, 2 * LANES), bf16)

    qkv_slots, kept = call(
        qkv_kernel,
        (shape((n_tp, rows, LANES), bf16), shape((2, 8, LANES), f32)),
        [HBM] * 4,
        scratch=[
            pltpu.VMEM(tokens.shape, bf16),
            pltpu.VMEM((1, tokens.shape[1]), f32),
            pltpu.VMEM(qkv_weight.shape[::-1], bf16),
            pltpu.SemaphoreType.DMA((4,)),
        ],
    )(*in_hbm(tokens, norm_attn.reshape(1, -1), qkv_weight.T, norm_mlp.reshape(8, LANES)))
    qkv_recv = lax.all_to_all(qkv_slots, "tp", 0, 0)

    gate = gate_weight.T
    up = up_weight.T
    loaded = call(
        load_kernel,
        (
            shape((4, rows, LANES), jnp.int32),
            shape((8, LANES), jnp.int32),
            shape((8, LANES), f32),
            shape(pool.shape, bf16),
            shape(prefix.shape, bf16),
            shape(mem.shape, f32),
            shape(out_weight.shape, bf16),
            shape(gate.shape, bf16),
            shape(up.shape, bf16),
            shape(down_weight.shape, bf16),
        ),
        [HBM] * 14,
        scratch=[
            pltpu.SMEM((rows,), jnp.int32),
            pltpu.SMEM((rows,), jnp.int32),
            pltpu.SMEM((rows,), jnp.int32),
            pltpu.SMEM(pages.shape, jnp.int32),
            pltpu.SMEM(out_slot.shape, jnp.int32),
            pltpu.SMEM(forget.shape, f32),
            pltpu.SMEM(write_rate.shape, f32),
            pltpu.SemaphoreType.DMA((7,)),
            pltpu.SemaphoreType.DMA((7,)),
        ],
    )(
        *in_hbm(lengths, prompt_group, span_close, pages, out_slot, forget, write_rate),
        *in_hbm(pool, prefix, mem, out_weight, gate, up, down_weight),
    )

    columns, marks, rates, pool_near, prefix_near, mem_near = loaded[:6]
    out_near, gate_near, up_near, down_near = loaded[6:]

    away, here, send = call(
        attend_kernel,
        (shape((rows, LANES), f32), shape((rows, LANES), f32), send_shape),
        [HBM] * 3 + [VMEM] * 6,
        scratch=[
            pltpu.SMEM(out_slot.shape, jnp.int32),
            pltpu.SMEM(move_dest.shape, jnp.int32),
            pltpu.SMEM(pages.shape, jnp.int32),
            pltpu.SemaphoreType.DMA((3,)),
        ],
    )(
        *in_hbm(out_slot, move_dest, pages),
        qkv_recv, columns, rates, pool_near, prefix_near, mem_near,
    )
    gathered = lax.all_gather(send, "rep", axis=0)
    away_recv = lax.ppermute(away, "tp", [(i, (i + n_tp // 2) % n_tp) for i in range(n_tp)])
    mem_after, recalled, pool_base = call(
        memory_kernel,
        (shape(mem.shape, f32), shape((rows, LANES), f32), shape(pool.shape, bf16)),
        [VMEM] * 5,
        out_specs=(VMEM, VMEM, HBM),
        scratch=[pltpu.VMEM((rows, rows * 64), f32), pltpu.SemaphoreType.DMA],
    )(qkv_recv, columns, rates, pool_near, mem_near)

    row_scratch = pltpu.VMEM((rows, 8, LANES), f32)
    terms = call(
        project_kernel, shape((n_tp, 8, LANES), bf16), [VMEM] * 4, scratch=[row_scratch]
    )(here, away_recv, recalled, out_near)
    terms_recv = lax.all_to_all(terms, "tp", 0, 0)

    hidden, normed_slots = call(
        hidden_kernel,
        (shape((8, LANES), f32), shape((n_tp, 8, LANES), bf16)),
        [VMEM] * 2,
    )(terms_recv, kept)
    normed_recv = lax.all_to_all(normed_slots, "tp", 0, 0)

    down_slots = call(
        mlp_kernel, shape((n_tp, 8, LANES), bf16), [VMEM] * 4, scratch=[row_scratch]
    )(normed_recv, gate_near, up_near, down_near)
    down_recv = lax.all_to_all(down_slots, "tp", 0, 0)

    row_slots = call(row_kernel, shape((n_tp, 8, LANES), bf16), [VMEM] * 2)(down_recv, hidden)
    rows_all = lax.all_to_all(row_slots, "tp", 0, 0)

    leaving = call(leave_kernel, shape((n_rep, 16, LANES), bf16), [VMEM] * 2)(marks, rows_all)
    arrived = lax.all_to_all(leaving, "rep", 0, 0)

    pool_out, mem_out, codes = call(
        place_kernel,
        (shape(pool.shape, bf16), shape(mem.shape, f32), shape((n_rep, 8, LANES), f32)),
        [HBM] * 5,
        out_specs=(HBM, HBM, VMEM),
        scratch=[
            pltpu.SMEM(pages.shape, jnp.int32),
            pltpu.SMEM(out_slot.shape, jnp.int32),
            pltpu.VMEM((n_rep, 8, LANES), bf16),
            pltpu.VMEM((2, LANES, 2 * LANES), bf16),
            pltpu.VMEM((2, 64, LANES), bf16),
            pltpu.VMEM((2, 64, LANES), f32),
            pltpu.SemaphoreType.DMA((3,)),
            pltpu.SemaphoreType.DMA((4,)),
            pltpu.SemaphoreType.DMA((2,)),
            pltpu.SemaphoreType.DMA((2,)),
        ],
        aliases={2: 0, 3: 1},
    )(*in_hbm(pages, out_slot, pool_base, mem_after, gathered))
    rows_out = call(
        rows_kernel, shape(tokens.shape, bf16), [VMEM] * 4, scratch=[row_scratch]
    )(marks, rows_all, arrived, codes)
    return rows_out, mem_out[:, None], pool_out[:, None]


def solution(mesh):
    placed = (
        P("rep", None),
        P("rep"),
        P("rep"),
        P("rep"),
        P("rep", None),
        P("rep", None),
        P("rep", None, None),
        P("rep", "tp", None, None),
        P(None, "tp", None, None),
        P("rep", "tp", None, None),
        P(),
        P(),
        P(None, "tp"),
        P("tp", None),
        P(None, "tp"),
        P(None, "tp"),
        P("tp", None),
        P(),
        P(),
    )
    return jax.shard_map(
        body,
        mesh=mesh,
        in_specs=placed,
        out_specs=(P("rep", None), P("rep", "tp", None, None), P("rep", "tp", None, None)),
        check_vma=False,
    )
```

```python
import jax
import jax.numpy as jnp
from jax import lax
from jax.experimental import pallas as pl
from jax.experimental.pallas import tpu as pltpu
from jax.sharding import PartitionSpec as P

f32 = jnp.float32
bf16 = jnp.bfloat16
highest = lax.Precision.HIGHEST
LANES = 128
NT = (((1,), (1,)), ((), ()))

VMEM = pl.BlockSpec(memory_space=pltpu.VMEM)
SMEM = pl.BlockSpec(memory_space=pltpu.SMEM)
HBM = pl.BlockSpec(memory_space=pltpu.MemorySpace.HBM)


def call(kernel, outs, in_specs, out_specs=None, scratch=(), aliases=None):
    return pl.pallas_call(
        kernel,
        out_shape=outs,
        in_specs=in_specs,
        out_specs=out_specs if out_specs is not None else jax.tree.map(lambda _: VMEM, outs),
        scratch_shapes=scratch,
        input_output_aliases=aliases or {},
        compiler_params=pltpu.CompilerParams(vmem_limit_bytes=24 << 20),
    )


def in_hbm(*arrays):
    return [pltpu.with_memory_space_constraint(a, pltpu.MemorySpace.HBM) for a in arrays]


def lane_ids(shape):
    return lax.broadcasted_iota(jnp.int32, shape, len(shape) - 1)


def row_ids(shape):
    return lax.broadcasted_iota(jnp.int32, shape, len(shape) - 2)


def column(read, count):
    rows = row_ids((count, LANES))
    out = jnp.zeros((count, LANES), jnp.int32)
    for r in range(count):
        out = jnp.where(rows == r, read(r), out)
    return out


def half_swap(block):
    return pltpu.roll(block, LANES // 2, 1)


def qkv_kernel(
    tokens_hbm, gain_hbm, weight_hbm, mlp_gain_hbm, out, kept, slices, tokens, gain, weight, sems
):
    loads = [
        pltpu.make_async_copy(tokens_hbm, tokens, sems.at[0]),
        pltpu.make_async_copy(gain_hbm, gain, sems.at[1]),
        pltpu.make_async_copy(mlp_gain_hbm, kept.at[1], sems.at[2]),
    ]
    part_rows = weight.shape[0] // 4
    for i in range(4):
        part = pl.ds(i * part_rows, part_rows)
        loads.append(pltpu.make_async_copy(weight_hbm.at[part], weight.at[part], sems.at[3 + i]))
    for load in loads:
        load.start()
    t = lax.axis_index("tp")
    loads[0].wait()
    loads[1].wait()
    x = tokens[...].astype(f32)
    row = jnp.sum(jnp.where(row_ids(x.shape) == t, x, 0.0), axis=0, keepdims=True)
    kept[0] = jnp.concatenate([row[:, k * LANES : (k + 1) * LANES] for k in range(8)], axis=0)
    mine = jnp.zeros(slices.shape, f32)
    for k in range(8):
        mine = jnp.where(t // 2 == k, x[:, k * LANES : (k + 1) * LANES], mine)
    slices[...] = jnp.where(lax.rem(t, 2) == 1, mine, half_swap(mine))
    scale = lax.rsqrt(jnp.mean(x * x, axis=-1, keepdims=True) + 1e-05)
    normed = (x * scale * gain[...]).astype(bf16)
    for load in loads[3:]:
        load.wait()
    part = lax.dot_general(normed, weight[...], NT, preferred_element_type=f32)
    part = part.astype(bf16).astype(f32)
    first = part[:, :LANES]
    last = part[:, LANES:]
    turned = half_swap(first)
    lanes = lane_ids(first.shape)
    low = lanes < 64
    blocks = (
        jnp.where(low, first, turned),
        jnp.where(low, turned, first),
        jnp.concatenate([last, last], axis=1),
    )
    placed = []
    for j, block in enumerate(blocks):
        sub = lax.rem(3 * t + j, 2)
        placed.append(jnp.where(lanes // 64 == sub, block, 0.0))
    for head in range(8):
        slot = jnp.zeros(first.shape, f32)
        for j in range(3):
            mine = lax.rem(3 * t + j, 16) // 2 == head
            slot = slot + jnp.where(mine, placed[j], 0.0)
        out[head] = slot.astype(bf16)
        out[head + 8] = slot.astype(bf16)
    loads[2].wait()


def load_kernel(
    lengths_hbm, groups_hbm, span_hbm, pages_hbm, slots_hbm, dests_hbm, forget_hbm, rate_hbm,
    pool_hbm, prefix_hbm, memory_hbm, weight_hbm, gate_hbm, up_hbm, down_hbm,
    columns, marks, rates, pool, prefix, memory, weight, gate, up, down, leaving, send_out,
    lengths, groups, span, pages, slots, dests, forget, rate, code, small_sems, sems, out_sems,
):
    small = [
        pltpu.make_async_copy(src, dst, small_sems.at[i])
        for i, (src, dst) in enumerate((
            (lengths_hbm, lengths), (groups_hbm, groups), (span_hbm, span), (pages_hbm, pages),
            (slots_hbm, slots), (dests_hbm, dests), (forget_hbm, forget), (rate_hbm, rate),
        ))
    ]
    big = [
        pltpu.make_async_copy(src, dst, sems.at[i])
        for i, (src, dst) in enumerate((
            (pool_hbm, pool), (prefix_hbm, prefix), (memory_hbm, memory), (weight_hbm, weight),
            (gate_hbm, gate), (up_hbm, up), (down_hbm, down),
        ))
    ]
    for load in small + big:
        load.start()
    t = lax.axis_index("tp")
    half = t // 8
    head = lax.rem(t, 8)
    rows = columns.shape[1]
    for load in small:
        load.wait()
    columns[0] = column(lambda r: lengths[r], rows)
    columns[1] = column(lambda r: groups[r], rows)
    columns[2] = column(lambda r: pages[half, r], rows)
    columns[3] = column(lambda r: span[r], rows)
    mark_row = row_ids(marks.shape)
    first = jnp.where(mark_row == 0, slots[0, 0], slots[0, 1])
    second = jnp.where(mark_row == 2, dests[0, 0], dests[0, 1])
    marks[...] = jnp.where(mark_row < 2, first, second)
    rates[...] = jnp.where(mark_row == 0, forget[head], rate[head])
    dest = jnp.where(row_ids(code.shape) == 0, dests[0, 0], dests[0, 1])
    code[...] = dest.astype(f32).astype(bf16)
    big[0].wait()
    stores = [
        pltpu.make_async_copy(code, send_out.at[pl.ds(2 * LANES + 64, 8)], out_sems.at[0])
    ]
    for m in range(2):
        page = pool.at[pages[half, slots[0, m]]]
        block = send_out.at[pl.ds(m * LANES, LANES)]
        stores.append(pltpu.make_async_copy(page, block, out_sems.at[1 + m]))
    for store in stores:
        store.start()
    big[2].wait()
    for m in range(2):
        leaving[m] = memory[slots[0, m]]
    for load in big[1:2] + big[3:]:
        load.wait()
    for store in stores:
        store.wait()


def pick(recv, kind, head):
    one = (16 * kind + 2 * head) // 3
    two = (16 * kind + 2 * head + 1) // 3
    a = recv[one].astype(f32)
    b = recv[two].astype(f32)
    return jnp.where(one == two, a, a + b)


def attend_kernel(
    recv, columns, rates, marks, pool, prefix, leaving, send_in,
    away_out, here_out, send_out,
    moving, send_sem,
):
    del send_in
    t = lax.axis_index("tp")
    half = t // 8
    head = lax.rem(t, 8)
    query = pick(recv, 0, head)
    key = pick(recv, 1, head)
    value = pick(recv, 2, head)
    rows = query.shape[0]
    lanes = lane_ids((rows, LANES))
    low = lanes < 64
    key_unit = key * lax.rsqrt(jnp.sum(key * key, axis=-1, keepdims=True) + 1e-06)
    value_half = jnp.where(half == 0, value, half_swap(value))
    row = row_ids(lanes.shape)
    mem_shape = leaving.shape[1:]
    diagonal = row_ids(mem_shape) == lane_ids(mem_shape)
    for m in range(2):
        mine = row == marks[m : m + 1]
        key_row = jnp.sum(jnp.where(mine, key_unit, 0.0), axis=0, keepdims=True)
        value_row = jnp.sum(jnp.where(mine, value_half, 0.0), axis=0, keepdims=True)
        closes = jnp.max(jnp.where(mine, columns[3], 0), axis=0, keepdims=True) == 1
        block = leaving[m]
        seen = jnp.sum(block * key_row, axis=1, keepdims=True)
        target = jnp.sum(jnp.where(diagonal, value_row, 0.0), axis=1, keepdims=True)
        written = rates[0:1] * block + rates[1:2] * (target - seen) * key_row
        written = jnp.where(closes, written, block)
        moving[:, m * LANES : (m + 1) * LANES] = written.astype(bf16)
    send = pltpu.make_async_copy(moving, send_out.at[pl.ds(2 * LANES, 64)], send_sem)
    send.start()
    length = columns[0]
    group = columns[1]
    page = columns[2]
    score_scale = LANES ** (-0.5)
    page_count = pool.shape[0]
    query_b = query.astype(bf16)
    pool_keys = pool[:, :, :LANES].reshape(page_count * LANES, LANES)
    pool_scores = lax.dot_general(query_b, pool_keys, NT, preferred_element_type=f32)
    pre_rows = prefix.shape[0] * prefix.shape[1]
    pre_keys = prefix[:, :, :LANES].reshape(pre_rows, LANES)
    pre_scores = lax.dot_general(query_b, pre_keys, NT, preferred_element_type=f32)
    tiles = []
    in_reach = lanes + half * LANES < length
    for p in range(page_count):
        live = (page == p) & in_reach
        tile = pool_scores[:, p * LANES : (p + 1) * LANES] * score_scale
        tiles.append(jnp.where(live, tile, -jnp.inf))
    for p in range(pre_rows // LANES):
        live = group == lanes // 64 + 2 * p
        tile = pre_scores[:, p * LANES : (p + 1) * LANES] * score_scale
        tiles.append(jnp.where(live, tile, -jnp.inf))
    own = jnp.sum(query * key, axis=-1, keepdims=True) * score_scale
    own = jnp.where(half == 0, own, -jnp.inf)
    peak = tiles[0]
    for tile in tiles[1:]:
        peak = jnp.maximum(peak, tile)
    top = jnp.maximum(jnp.max(peak, axis=-1, keepdims=True), own)
    weights = [jnp.exp(tile - top) for tile in tiles]
    own_weight = jnp.exp(own - top)
    total = weights[0]
    for tile in weights[1:]:
        total = total + tile
    denom = jnp.sum(total, axis=-1, keepdims=True) + own_weight

    def both(parts):
        full = jnp.concatenate(parts, axis=1)
        upper = full.astype(bf16)
        lower = (full - upper.astype(f32)).astype(bf16)
        return jnp.concatenate([upper, lower], axis=0)

    pool_values = pool[:, :, LANES:].reshape(page_count * LANES, LANES)
    pre_values = prefix[:, :, LANES:].reshape(pre_rows, LANES)
    summed = jnp.dot(both(weights[:page_count]), pool_values, preferred_element_type=f32)
    summed = summed + jnp.dot(
        both(weights[page_count:]), pre_values, preferred_element_type=f32
    )
    summed = summed[:rows] + summed[rows:] + own_weight * value
    attended = summed / denom
    lse = top + jnp.log(denom)
    swapped = half_swap(attended)
    here_out[...] = jnp.where(low, jnp.where(half == 0, attended, swapped), lse)
    away_out[...] = jnp.where(low, jnp.where(half == 0, swapped, attended), lse)
    send.wait()


def memory_kernel(
    recv, columns, rates, pool, memory, memory_out, recalled_out, pool_out, masked, out_sem
):
    pool_copy = pltpu.make_async_copy(pool, pool_out, out_sem)
    pool_copy.start()
    t = lax.axis_index("tp")
    half = t // 8
    head = lax.rem(t, 8)
    query = pick(recv, 0, head)
    key = pick(recv, 1, head)
    value = pick(recv, 2, head)
    rows = query.shape[0]
    shape = query.shape
    lanes = lane_ids(shape)
    row = row_ids(shape)
    low = lanes < 64
    query_unit = query * lax.rsqrt(jnp.sum(query * query, axis=-1, keepdims=True) + 1e-06)
    key_unit = key * lax.rsqrt(jnp.sum(key * key, axis=-1, keepdims=True) + 1e-06)
    mem_rows = memory.shape[1]
    flat_memory = memory[...].reshape(rows * mem_rows, LANES)
    seen = lax.dot_general(
        jnp.concatenate([query_unit, key_unit], axis=0), flat_memory, NT,
        preferred_element_type=f32, precision=highest,
    )
    recalled = jnp.zeros(shape, f32)
    value_half = jnp.where(half == 0, value, half_swap(value))
    value_both = jnp.where(low, value_half, half_swap(value_half))
    closing = columns[3] == 1
    keep = rates[0:1]
    step = rates[1:2]
    for c in range(rows // 2):
        mine = row == 2 * c + lanes // 64
        cut = slice(c * LANES, (c + 1) * LANES)
        recalled = recalled + jnp.where(mine, seen[:rows, cut], 0.0)
        misfit = (value_both - seen[rows:, cut]) * step
        masked[:, cut] = jnp.where(mine & closing, misfit, 0.0)
    recalled_out[...] = recalled + half_swap(recalled)
    change = lax.dot_general(
        masked[...], key_unit, (((0,), (0,)), ((), ())),
        preferred_element_type=f32, precision=highest,
    )
    decay = jnp.where(closing, keep, 1.0)
    for r in range(rows):
        memory_out[r] = decay[r : r + 1] * memory[r] + change[r * mem_rows : (r + 1) * mem_rows]
    pool_copy.wait()


def spread(rows, wide):
    for k in range(8):
        rows[:, k, :] = wide[:, k * LANES : (k + 1) * LANES]


def join_kernel(here, away, recalled, slices, marks, mixed_out, out):
    mine = here[...]
    other = away[...]
    lse = mine[:, 64:65]
    lse_other = other[:, 64:65]
    share = 1.0 / (1.0 + jnp.exp(lse_other - lse))
    share_other = 1.0 / (1.0 + jnp.exp(lse - lse_other))
    mixed = share * mine + share_other * other + recalled[...]
    mixed = jnp.where(lane_ids(mixed.shape) < 64, mixed, slices[...])
    mixed_out[...] = mixed
    row = row_ids(mixed.shape)
    parts = []
    for m in range(2):
        parts.append(jnp.sum(jnp.where(row == marks[m : m + 1], mixed, 0.0), axis=0, keepdims=True))
    parts.append(marks[2:8].astype(f32))
    block = jnp.concatenate(parts, axis=0).astype(bf16)
    for s in range(out.shape[0]):
        out[s] = block


def project_kernel(mixed_in, arrived, marks, weight, out, rows, came):
    t = lax.axis_index("tp")
    me = lax.axis_index("rep").astype(f32)
    came[...] = arrived[...].astype(f32)
    mixed = mixed_in[...]
    row = row_ids(mixed.shape)
    extra = jnp.zeros(mixed.shape, f32)
    for m in range(2):
        match = came[:, 2 + m, :] == me
        entry = jnp.sum(jnp.where(match, came[:, m, :], 0.0), axis=0, keepdims=True)
        here = row == marks[m : m + 1]
        mixed = jnp.where(here, entry, mixed)
        extra = jnp.where(here, entry, extra)
    low = lane_ids(extra.shape) < 64
    odd = lax.rem(t, 2) == 1
    extra = jnp.where(low, jnp.where(odd, 0.0, half_swap(extra)), jnp.where(odd, extra, 0.0))
    wide = jnp.dot(mixed.astype(bf16)[:, :64], weight[...], preferred_element_type=f32)
    for k in range(8):
        tile = wide[:, k * LANES : (k + 1) * LANES]
        rows[:, k, :] = tile + jnp.where(t // 2 == k, extra, 0.0)
    out[...] = rows[...].astype(bf16)


def hidden_kernel(recv, kept, marks, hidden_out, normed_out):
    t = lax.axis_index("tp")
    taken = (marks[0:1] == t) | (marks[1:2] == t)
    hidden = jnp.where(taken, 0.0, kept[0])
    for s in range(recv.shape[0]):
        hidden = hidden + recv[s].astype(f32)
    hidden_out[...] = hidden
    square = jnp.sum(jnp.sum(hidden * hidden, axis=1, keepdims=True), axis=0, keepdims=True)
    scale = lax.rsqrt(square / (8 * LANES) + 1e-05)
    normed = (hidden * scale * kept[1]).astype(bf16)
    for s in range(normed_out.shape[0]):
        normed_out[s] = normed


def mlp_kernel(recv, gate_weight, up_weight, down_weight, out, rows):
    rows[...] = recv[...].astype(f32)
    x = jnp.concatenate([rows[:, k, :] for k in range(8)], axis=1).astype(bf16)
    gate = lax.dot_general(x, gate_weight[...], NT, preferred_element_type=f32)
    up = lax.dot_general(x, up_weight[...], NT, preferred_element_type=f32)
    active = (gate * (1.0 / (1.0 + jnp.exp(-gate))) * up).astype(bf16)
    spread(rows, jnp.dot(active, down_weight[...], preferred_element_type=f32))
    out[...] = rows[...].astype(bf16)


def row_kernel(recv, hidden, out):
    total = hidden[...]
    for s in range(recv.shape[0]):
        total = total + recv[s].astype(f32)
    row = total.astype(bf16)
    for s in range(16):
        out[s] = row


def place_kernel(
    pages_hbm, slots_hbm, pool, memory, gathered, pool_out, memory_out, codes_out,
    pages, slots, codes, page, raw, wide, small_sems, page_sem, raw_sem, wide_sem,
):
    small = [
        pltpu.make_async_copy(pages_hbm, pages, small_sems.at[0]),
        pltpu.make_async_copy(slots_hbm, slots, small_sems.at[1]),
        pltpu.make_async_copy(
            gathered.at[:, pl.ds(2 * LANES + 64, 8), pl.ds(0, LANES)], codes, small_sems.at[2]
        ),
    ]
    for load in small:
        load.start()
    half = lax.axis_index("tp") // 8
    me = lax.axis_index("rep").astype(f32)
    for load in small:
        load.wait()
    all_codes = codes[...].astype(f32)
    codes_out[...] = all_codes
    row = row_ids((codes.shape[0], LANES))
    moved = []
    for m in range(2):
        source = jnp.max(jnp.where(codes_out[:, m, :] == me, row, 0))
        page_in = pltpu.make_async_copy(
            gathered.at[source, pl.ds(m * LANES, LANES), :], page.at[m], page_sem.at[m]
        )
        raw_in = pltpu.make_async_copy(
            gathered.at[source, pl.ds(2 * LANES, 64), pl.ds(m * LANES, LANES)],
            raw.at[m],
            raw_sem.at[m],
        )
        page_in.start()
        raw_in.start()
        moved.append((page_in, raw_in))
    stores = []
    for m in range(2):
        moved[m][0].wait()
        place = pool_out.at[pages[half, slots[0, m]]]
        stores.append(pltpu.make_async_copy(page.at[m], place, page_sem.at[2 + m]))
        stores[-1].start()
    for m in range(2):
        moved[m][1].wait()
        wide[m] = raw[m].astype(f32)
        place = memory_out.at[slots[0, m]]
        stores.append(pltpu.make_async_copy(wide.at[m], place, wide_sem.at[m]))
        stores[-1].start()
    for store in stores:
        store.wait()


def rows_kernel(rows_all, codes, rows_out, rows):
    del codes
    rows[...] = rows_all[...].astype(f32)
    for k in range(8):
        rows_out[:, k * LANES : (k + 1) * LANES] = rows[:, k, :].astype(bf16)


def body(
    tokens,
    lengths,
    prompt_group,
    span_close,
    out_slot,
    move_dest,
    page_table,
    cache_pool,
    prefix_cache,
    memory,
    norm_attn,
    norm_mlp,
    qkv_weight,
    out_weight,
    gate_weight,
    up_weight,
    down_weight,
    forget,
    write_rate,
):
    shape = jax.ShapeDtypeStruct
    rows = tokens.shape[0]
    n_tp = lax.axis_size("tp")
    n_rep = lax.axis_size("rep")
    pages = page_table.transpose(2, 1, 0)[0]
    pool = cache_pool[:, 0]
    prefix = prefix_cache[:, 0]
    mem = memory[:, 0]
    send_shape = shape((2 * LANES + 72, 2 * LANES), bf16)

    qkv_slots, kept, slices = call(
        qkv_kernel,
        (
            shape((n_tp, rows, LANES), bf16),
            shape((2, 8, LANES), f32),
            shape((rows, LANES), f32),
        ),
        [HBM] * 4,
        scratch=[
            pltpu.VMEM(tokens.shape, bf16),
            pltpu.VMEM((1, tokens.shape[1]), f32),
            pltpu.VMEM(qkv_weight.shape[::-1], bf16),
            pltpu.SemaphoreType.DMA((7,)),
        ],
    )(*in_hbm(tokens, norm_attn.reshape(1, -1), qkv_weight.T, norm_mlp.reshape(8, LANES)))
    qkv_recv = lax.all_to_all(qkv_slots, "tp", 0, 0)

    gate = gate_weight.T
    up = up_weight.T
    loaded = call(
        load_kernel,
        (
            shape((4, rows, LANES), jnp.int32),
            shape((8, LANES), jnp.int32),
            shape((8, LANES), f32),
            shape(pool.shape, bf16),
            shape(prefix.shape, bf16),
            shape(mem.shape, f32),
            shape(out_weight.shape, bf16),
            shape(gate.shape, bf16),
            shape(up.shape, bf16),
            shape(down_weight.shape, bf16),
            shape((2,) + mem.shape[1:], f32),
            send_shape,
        ),
        [HBM] * 15,
        out_specs=(VMEM,) * 11 + (HBM,),
        scratch=[
            pltpu.SMEM((rows,), jnp.int32),
            pltpu.SMEM((rows,), jnp.int32),
            pltpu.SMEM((rows,), jnp.int32),
            pltpu.SMEM(pages.shape, jnp.int32),
            pltpu.SMEM(out_slot.shape, jnp.int32),
            pltpu.SMEM(move_dest.shape, jnp.int32),
            pltpu.SMEM(forget.shape, f32),
            pltpu.SMEM(write_rate.shape, f32),
            pltpu.VMEM((8, 2 * LANES), bf16),
            pltpu.SemaphoreType.DMA((8,)),
            pltpu.SemaphoreType.DMA((7,)),
            pltpu.SemaphoreType.DMA((3,)),
        ],
    )(
        *in_hbm(lengths, prompt_group, span_close, pages, out_slot, move_dest, forget, write_rate),
        *in_hbm(pool, prefix, mem, out_weight, gate, up, down_weight),
    )

    columns, marks, rates, pool_near, prefix_near, mem_near = loaded[:6]
    out_near, gate_near, up_near, down_near, leaving_mem, send = loaded[6:]

    away, here, send = call(
        attend_kernel,
        (shape((rows, LANES), f32), shape((rows, LANES), f32), send_shape),
        [VMEM] * 7 + [HBM],
        out_specs=(VMEM, VMEM, HBM),
        scratch=[pltpu.VMEM((64, 2 * LANES), bf16), pltpu.SemaphoreType.DMA],
        aliases={7: 2},
    )(
        qkv_recv, columns, rates, marks, pool_near, prefix_near, leaving_mem, *in_hbm(send)
    )
    gathered = lax.all_gather(send, "rep", axis=0)
    away_recv = lax.ppermute(away, "tp", [(i, (i + n_tp // 2) % n_tp) for i in range(n_tp)])
    mem_after, recalled, pool_base = call(
        memory_kernel,
        (shape(mem.shape, f32), shape((rows, LANES), f32), shape(pool.shape, bf16)),
        [VMEM] * 5,
        out_specs=(VMEM, VMEM, HBM),
        scratch=[pltpu.VMEM((rows, rows * 64), f32), pltpu.SemaphoreType.DMA],
    )(qkv_recv, columns, rates, pool_near, mem_near)

    row_scratch = pltpu.VMEM((rows, 8, LANES), f32)
    mixed, leaving = call(
        join_kernel, (shape((rows, LANES), f32), shape((n_rep, 8, LANES), bf16)), [VMEM] * 5
    )(here, away_recv, recalled, slices, marks)
    arrived = lax.all_to_all(leaving, "rep", 0, 0)
    terms = call(
        project_kernel,
        shape((n_tp, 8, LANES), bf16),
        [VMEM] * 4,
        scratch=[row_scratch, pltpu.VMEM((n_rep, 8, LANES), f32)],
    )(mixed, arrived, marks, out_near)
    terms_recv = lax.all_to_all(terms, "tp", 0, 0)

    hidden, normed_slots = call(
        hidden_kernel,
        (shape((8, LANES), f32), shape((n_tp, 8, LANES), bf16)),
        [VMEM] * 3,
    )(terms_recv, kept, marks)
    normed_recv = lax.all_to_all(normed_slots, "tp", 0, 0)

    down_slots = call(
        mlp_kernel, shape((n_tp, 8, LANES), bf16), [VMEM] * 4, scratch=[row_scratch]
    )(normed_recv, gate_near, up_near, down_near)
    down_recv = lax.all_to_all(down_slots, "tp", 0, 0)

    row_slots = call(row_kernel, shape((n_tp, 8, LANES), bf16), [VMEM] * 2)(down_recv, hidden)
    rows_all = lax.all_to_all(row_slots, "tp", 0, 0)

    pool_out, mem_out, codes = call(
        place_kernel,
        (shape(pool.shape, bf16), shape(mem.shape, f32), shape((n_rep, 8, LANES), f32)),
        [HBM] * 5,
        out_specs=(HBM, HBM, VMEM),
        scratch=[
            pltpu.SMEM(pages.shape, jnp.int32),
            pltpu.SMEM(out_slot.shape, jnp.int32),
            pltpu.VMEM((n_rep, 8, LANES), bf16),
            pltpu.VMEM((2, LANES, 2 * LANES), bf16),
            pltpu.VMEM((2, 64, LANES), bf16),
            pltpu.VMEM((2, 64, LANES), f32),
            pltpu.SemaphoreType.DMA((3,)),
            pltpu.SemaphoreType.DMA((4,)),
            pltpu.SemaphoreType.DMA((2,)),
            pltpu.SemaphoreType.DMA((2,)),
        ],
        aliases={2: 0, 3: 1},
    )(*in_hbm(pages, out_slot, pool_base, mem_after, gathered))
    rows_out = call(
        rows_kernel, shape(tokens.shape, bf16), [VMEM] * 2, scratch=[row_scratch]
    )(rows_all, codes)
    return rows_out, mem_out[:, None], pool_out[:, None]


def solution(mesh):
    placed = (
        P("rep", None),
        P("rep"),
        P("rep"),
        P("rep"),
        P("rep", None),
        P("rep", None),
        P("rep", None, None),
        P("rep", "tp", None, None),
        P(None, "tp", None, None),
        P("rep", "tp", None, None),
        P(),
        P(),
        P(None, "tp"),
        P("tp", None),
        P(None, "tp"),
        P(None, "tp"),
        P("tp", None),
        P(),
        P(),
    )
    return jax.shard_map(
        body,
        mesh=mesh,
        in_specs=placed,
        out_specs=(P("rep", None), P("rep", "tp", None, None), P("rep", "tp", None, None)),
        check_vma=False,
    )
```

```python
import jax
import jax.numpy as jnp
from jax import lax
from jax.experimental import pallas as pl
from jax.experimental.pallas import tpu as pltpu
from jax.sharding import PartitionSpec as P

f32 = jnp.float32
bf16 = jnp.bfloat16
highest = lax.Precision.HIGHEST
LANES = 128
NT = (((1,), (1,)), ((), ()))

VMEM = pl.BlockSpec(memory_space=pltpu.VMEM)
SMEM = pl.BlockSpec(memory_space=pltpu.SMEM)
HBM = pl.BlockSpec(memory_space=pltpu.MemorySpace.HBM)


def call(kernel, outs, in_specs, out_specs=None, scratch=(), aliases=None):
    return pl.pallas_call(
        kernel,
        out_shape=outs,
        in_specs=in_specs,
        out_specs=out_specs if out_specs is not None else jax.tree.map(lambda _: VMEM, outs),
        scratch_shapes=scratch,
        input_output_aliases=aliases or {},
        compiler_params=pltpu.CompilerParams(vmem_limit_bytes=24 << 20),
    )


def in_hbm(*arrays):
    return [pltpu.with_memory_space_constraint(a, pltpu.MemorySpace.HBM) for a in arrays]


def lane_ids(shape):
    return lax.broadcasted_iota(jnp.int32, shape, len(shape) - 1)


def row_ids(shape):
    return lax.broadcasted_iota(jnp.int32, shape, len(shape) - 2)


def column(read, count):
    rows = row_ids((count, LANES))
    out = jnp.zeros((count, LANES), jnp.int32)
    for r in range(count):
        out = jnp.where(rows == r, read(r), out)
    return out


def half_swap(block):
    return pltpu.roll(block, LANES // 2, 1)


def qkv_kernel(
    tokens_hbm, gain_hbm, weight_hbm, mlp_gain_hbm, out, kept, slices, tokens, gain, weight, sems
):
    loads = [
        pltpu.make_async_copy(tokens_hbm, tokens, sems.at[0]),
        pltpu.make_async_copy(gain_hbm, gain, sems.at[1]),
        pltpu.make_async_copy(mlp_gain_hbm, kept.at[1], sems.at[2]),
    ]
    width = weight.shape[2]
    for i in range(4):
        piece = weight_hbm.at[:, pl.ds(i * width, width)]
        loads.append(pltpu.make_async_copy(piece, weight.at[i], sems.at[3 + i]))
    for load in loads:
        load.start()
    t = lax.axis_index("tp")
    loads[0].wait()
    loads[1].wait()
    x = tokens[...].astype(f32)
    row = jnp.sum(jnp.where(row_ids(x.shape) == t, x, 0.0), axis=0, keepdims=True)
    kept[0] = jnp.concatenate([row[:, k * LANES : (k + 1) * LANES] for k in range(8)], axis=0)
    mine = jnp.zeros(slices.shape, f32)
    for k in range(8):
        mine = jnp.where(t // 2 == k, x[:, k * LANES : (k + 1) * LANES], mine)
    slices[...] = jnp.where(lax.rem(t, 2) == 1, mine, half_swap(mine))
    scale = lax.rsqrt(jnp.mean(x * x, axis=-1, keepdims=True) + 1e-05)
    normed = (x * scale * gain[...]).astype(bf16)
    part = jnp.zeros((x.shape[0], weight.shape[1]), f32)
    for i in range(4):
        loads[3 + i].wait()
        cut = normed[:, i * width : (i + 1) * width]
        part = part + lax.dot_general(cut, weight[i], NT, preferred_element_type=f32)
    part = part.astype(bf16).astype(f32)
    first = part[:, :LANES]
    last = part[:, LANES:]
    turned = half_swap(first)
    lanes = lane_ids(first.shape)
    low = lanes < 64
    blocks = (
        jnp.where(low, first, turned),
        jnp.where(low, turned, first),
        jnp.concatenate([last, last], axis=1),
    )
    placed = []
    for j, block in enumerate(blocks):
        sub = lax.rem(3 * t + j, 2)
        placed.append(jnp.where(lanes // 64 == sub, block, 0.0))
    for head in range(8):
        slot = jnp.zeros(first.shape, f32)
        for j in range(3):
            mine = lax.rem(3 * t + j, 16) // 2 == head
            slot = slot + jnp.where(mine, placed[j], 0.0)
        out[head] = slot.astype(bf16)
        out[head + 8] = slot.astype(bf16)
    loads[2].wait()


def load_kernel(
    lengths_hbm, groups_hbm, span_hbm, pages_hbm, slots_hbm, dests_hbm, forget_hbm, rate_hbm,
    pool_hbm, prefix_hbm, memory_hbm, weight_hbm, gate_hbm, up_hbm, down_hbm,
    columns, marks, rates, pool, prefix, memory, weight, gate, up, down, leaving, send_out,
    lengths, groups, span, pages, slots, dests, forget, rate, code, small_sems, sems, out_sems,
):
    small = [
        pltpu.make_async_copy(src, dst, small_sems.at[i])
        for i, (src, dst) in enumerate((
            (lengths_hbm, lengths), (groups_hbm, groups), (span_hbm, span), (pages_hbm, pages),
            (slots_hbm, slots), (dests_hbm, dests), (forget_hbm, forget), (rate_hbm, rate),
        ))
    ]
    big = [
        pltpu.make_async_copy(src, dst, sems.at[i])
        for i, (src, dst) in enumerate((
            (pool_hbm, pool), (prefix_hbm, prefix), (memory_hbm, memory), (weight_hbm, weight),
            (gate_hbm, gate), (up_hbm, up), (down_hbm, down),
        ))
    ]
    for load in small + big:
        load.start()
    t = lax.axis_index("tp")
    half = t // 8
    head = lax.rem(t, 8)
    rows = columns.shape[1]
    for load in small:
        load.wait()
    columns[0] = column(lambda r: lengths[r], rows)
    columns[1] = column(lambda r: groups[r], rows)
    columns[2] = column(lambda r: pages[half, r], rows)
    columns[3] = column(lambda r: span[r], rows)
    mark_row = row_ids(marks.shape)
    first = jnp.where(mark_row == 0, slots[0, 0], slots[0, 1])
    second = jnp.where(mark_row == 2, dests[0, 0], dests[0, 1])
    marks[...] = jnp.where(mark_row < 2, first, second)
    rates[...] = jnp.where(mark_row == 0, forget[head], rate[head])
    dest = jnp.where(row_ids(code.shape) == 0, dests[0, 0], dests[0, 1])
    code[...] = dest.astype(f32).astype(bf16)
    big[0].wait()
    stores = [
        pltpu.make_async_copy(code, send_out.at[pl.ds(2 * LANES + 64, 8)], out_sems.at[0])
    ]
    for m in range(2):
        page = pool.at[pages[half, slots[0, m]]]
        block = send_out.at[pl.ds(m * LANES, LANES)]
        stores.append(pltpu.make_async_copy(page, block, out_sems.at[1 + m]))
    for store in stores:
        store.start()
    big[2].wait()
    for m in range(2):
        leaving[m] = memory[slots[0, m]]
    for load in big[1:2] + big[3:]:
        load.wait()
    for store in stores:
        store.wait()


def pick(recv, kind, head):
    one = (16 * kind + 2 * head) // 3
    two = (16 * kind + 2 * head + 1) // 3
    a = recv[one].astype(f32)
    b = recv[two].astype(f32)
    return jnp.where(one == two, a, a + b)


def attend_kernel(
    recv, columns, rates, marks, pool, prefix, leaving, send_in,
    away_out, here_out, send_out,
    moving, send_sem,
):
    del send_in
    t = lax.axis_index("tp")
    half = t // 8
    head = lax.rem(t, 8)
    query = pick(recv, 0, head)
    key = pick(recv, 1, head)
    value = pick(recv, 2, head)
    rows = query.shape[0]
    lanes = lane_ids((rows, LANES))
    low = lanes < 64
    key_unit = key * lax.rsqrt(jnp.sum(key * key, axis=-1, keepdims=True) + 1e-06)
    value_half = jnp.where(half == 0, value, half_swap(value))
    row = row_ids(lanes.shape)
    mem_shape = leaving.shape[1:]
    diagonal = row_ids(mem_shape) == lane_ids(mem_shape)
    for m in range(2):
        mine = row == marks[m : m + 1]
        key_row = jnp.sum(jnp.where(mine, key_unit, 0.0), axis=0, keepdims=True)
        value_row = jnp.sum(jnp.where(mine, value_half, 0.0), axis=0, keepdims=True)
        closes = jnp.max(jnp.where(mine, columns[3], 0), axis=0, keepdims=True) == 1
        block = leaving[m]
        seen = jnp.sum(block * key_row, axis=1, keepdims=True)
        target = jnp.sum(jnp.where(diagonal, value_row, 0.0), axis=1, keepdims=True)
        written = rates[0:1] * block + rates[1:2] * (target - seen) * key_row
        written = jnp.where(closes, written, block)
        moving[:, m * LANES : (m + 1) * LANES] = written.astype(bf16)
    send = pltpu.make_async_copy(moving, send_out.at[pl.ds(2 * LANES, 64)], send_sem)
    send.start()
    length = columns[0]
    group = columns[1]
    page = columns[2]
    score_scale = LANES ** (-0.5)
    page_count = pool.shape[0]
    query_b = query.astype(bf16)
    pool_keys = pool[:, :, :LANES].reshape(page_count * LANES, LANES)
    pool_scores = lax.dot_general(query_b, pool_keys, NT, preferred_element_type=f32)
    pre_rows = prefix.shape[0] * prefix.shape[1]
    pre_keys = prefix[:, :, :LANES].reshape(pre_rows, LANES)
    pre_scores = lax.dot_general(query_b, pre_keys, NT, preferred_element_type=f32)
    tiles = []
    in_reach = lanes + half * LANES < length
    for p in range(page_count):
        live = (page == p) & in_reach
        tile = pool_scores[:, p * LANES : (p + 1) * LANES] * score_scale
        tiles.append(jnp.where(live, tile, -jnp.inf))
    for p in range(pre_rows // LANES):
        live = group == lanes // 64 + 2 * p
        tile = pre_scores[:, p * LANES : (p + 1) * LANES] * score_scale
        tiles.append(jnp.where(live, tile, -jnp.inf))
    own = jnp.sum(query * key, axis=-1, keepdims=True) * score_scale
    own = jnp.where(half == 0, own, -jnp.inf)
    peak = tiles[0]
    for tile in tiles[1:]:
        peak = jnp.maximum(peak, tile)
    top = jnp.maximum(jnp.max(peak, axis=-1, keepdims=True), own)
    weights = [jnp.exp(tile - top) for tile in tiles]
    own_weight = jnp.exp(own - top)
    total = weights[0]
    for tile in weights[1:]:
        total = total + tile
    denom = jnp.sum(total, axis=-1, keepdims=True) + own_weight

    def both(parts):
        full = jnp.concatenate(parts, axis=1)
        upper = full.astype(bf16)
        lower = (full - upper.astype(f32)).astype(bf16)
        return jnp.concatenate([upper, lower], axis=0)

    pool_values = pool[:, :, LANES:].reshape(page_count * LANES, LANES)
    pre_values = prefix[:, :, LANES:].reshape(pre_rows, LANES)
    summed = jnp.dot(both(weights[:page_count]), pool_values, preferred_element_type=f32)
    summed = summed + jnp.dot(
        both(weights[page_count:]), pre_values, preferred_element_type=f32
    )
    summed = summed[:rows] + summed[rows:] + own_weight * value
    attended = summed / denom
    lse = top + jnp.log(denom)
    swapped = half_swap(attended)
    here_out[...] = jnp.where(low, jnp.where(half == 0, attended, swapped), lse)
    away_out[...] = jnp.where(low, jnp.where(half == 0, swapped, attended), lse)
    send.wait()


def memory_kernel(
    recv, columns, rates, pool, memory, memory_out, recalled_out, pool_out, masked, out_sem
):
    pool_copy = pltpu.make_async_copy(pool, pool_out, out_sem)
    pool_copy.start()
    t = lax.axis_index("tp")
    half = t // 8
    head = lax.rem(t, 8)
    query = pick(recv, 0, head)
    key = pick(recv, 1, head)
    value = pick(recv, 2, head)
    rows = query.shape[0]
    shape = query.shape
    lanes = lane_ids(shape)
    row = row_ids(shape)
    low = lanes < 64
    query_unit = query * lax.rsqrt(jnp.sum(query * query, axis=-1, keepdims=True) + 1e-06)
    key_unit = key * lax.rsqrt(jnp.sum(key * key, axis=-1, keepdims=True) + 1e-06)
    mem_rows = memory.shape[1]
    flat_memory = memory[...].reshape(rows * mem_rows, LANES)
    seen = lax.dot_general(
        jnp.concatenate([query_unit, key_unit], axis=0), flat_memory, NT,
        preferred_element_type=f32, precision=highest,
    )
    recalled = jnp.zeros(shape, f32)
    value_half = jnp.where(half == 0, value, half_swap(value))
    value_both = jnp.where(low, value_half, half_swap(value_half))
    closing = columns[3] == 1
    keep = rates[0:1]
    step = rates[1:2]
    for c in range(rows // 2):
        mine = row == 2 * c + lanes // 64
        cut = slice(c * LANES, (c + 1) * LANES)
        recalled = recalled + jnp.where(mine, seen[:rows, cut], 0.0)
        misfit = (value_both - seen[rows:, cut]) * step
        masked[:, cut] = jnp.where(mine & closing, misfit, 0.0)
    recalled_out[...] = recalled + half_swap(recalled)
    change = lax.dot_general(
        masked[...], key_unit, (((0,), (0,)), ((), ())),
        preferred_element_type=f32, precision=highest,
    )
    decay = jnp.where(closing, keep, 1.0)
    for r in range(rows):
        memory_out[r] = decay[r : r + 1] * memory[r] + change[r * mem_rows : (r + 1) * mem_rows]
    pool_copy.wait()


def spread(rows, wide):
    for k in range(8):
        rows[:, k, :] = wide[:, k * LANES : (k + 1) * LANES]


def join_kernel(here, away, recalled, slices, marks, mixed_out, out):
    mine = here[...]
    other = away[...]
    lse = mine[:, 64:65]
    lse_other = other[:, 64:65]
    share = 1.0 / (1.0 + jnp.exp(lse_other - lse))
    share_other = 1.0 / (1.0 + jnp.exp(lse - lse_other))
    mixed = share * mine + share_other * other + recalled[...]
    mixed = jnp.where(lane_ids(mixed.shape) < 64, mixed, slices[...])
    mixed_out[...] = mixed
    row = row_ids(mixed.shape)
    parts = []
    for m in range(2):
        parts.append(jnp.sum(jnp.where(row == marks[m : m + 1], mixed, 0.0), axis=0, keepdims=True))
    parts.append(marks[2:8].astype(f32))
    block = jnp.concatenate(parts, axis=0).astype(bf16)
    for s in range(out.shape[0]):
        out[s] = block


def project_kernel(mixed_in, arrived, marks, weight, out, rows, came):
    t = lax.axis_index("tp")
    me = lax.axis_index("rep").astype(f32)
    came[...] = arrived[...].astype(f32)
    mixed = mixed_in[...]
    row = row_ids(mixed.shape)
    extra = jnp.zeros(mixed.shape, f32)
    for m in range(2):
        match = came[:, 2 + m, :] == me
        entry = jnp.sum(jnp.where(match, came[:, m, :], 0.0), axis=0, keepdims=True)
        here = row == marks[m : m + 1]
        mixed = jnp.where(here, entry, mixed)
        extra = jnp.where(here, entry, extra)
    low = lane_ids(extra.shape) < 64
    odd = lax.rem(t, 2) == 1
    extra = jnp.where(low, jnp.where(odd, 0.0, half_swap(extra)), jnp.where(odd, extra, 0.0))
    wide = jnp.dot(mixed.astype(bf16)[:, :64], weight[...], preferred_element_type=f32)
    for k in range(8):
        tile = wide[:, k * LANES : (k + 1) * LANES]
        rows[:, k, :] = tile + jnp.where(t // 2 == k, extra, 0.0)
    out[...] = rows[...].astype(bf16)


def hidden_kernel(recv, kept, marks, hidden_out, normed_out):
    t = lax.axis_index("tp")
    taken = (marks[0:1] == t) | (marks[1:2] == t)
    hidden = jnp.where(taken, 0.0, kept[0])
    for s in range(recv.shape[0]):
        hidden = hidden + recv[s].astype(f32)
    hidden_out[...] = hidden
    square = jnp.sum(jnp.sum(hidden * hidden, axis=1, keepdims=True), axis=0, keepdims=True)
    scale = lax.rsqrt(square / (8 * LANES) + 1e-05)
    normed = (hidden * scale * kept[1]).astype(bf16)
    for s in range(normed_out.shape[0]):
        normed_out[s] = normed


def mlp_kernel(recv, gate_weight, up_weight, down_weight, out, rows):
    rows[...] = recv[...].astype(f32)
    x = jnp.concatenate([rows[:, k, :] for k in range(8)], axis=1).astype(bf16)
    gate = lax.dot_general(x, gate_weight[...], NT, preferred_element_type=f32)
    up = lax.dot_general(x, up_weight[...], NT, preferred_element_type=f32)
    active = (gate * (1.0 / (1.0 + jnp.exp(-gate))) * up).astype(bf16)
    spread(rows, jnp.dot(active, down_weight[...], preferred_element_type=f32))
    out[...] = rows[...].astype(bf16)


def row_kernel(recv, hidden, out):
    total = hidden[...]
    for s in range(recv.shape[0]):
        total = total + recv[s].astype(f32)
    row = total.astype(bf16)
    for s in range(16):
        out[s] = row


def place_kernel(
    pages_hbm, slots_hbm, pool, memory, gathered, pool_out, memory_out, codes_out,
    pages, slots, codes, page, raw, wide, small_sems, page_sem, raw_sem, wide_sem,
):
    small = [
        pltpu.make_async_copy(pages_hbm, pages, small_sems.at[0]),
        pltpu.make_async_copy(slots_hbm, slots, small_sems.at[1]),
        pltpu.make_async_copy(
            gathered.at[:, pl.ds(2 * LANES + 64, 8), pl.ds(0, LANES)], codes, small_sems.at[2]
        ),
    ]
    for load in small:
        load.start()
    half = lax.axis_index("tp") // 8
    me = lax.axis_index("rep").astype(f32)
    for load in small:
        load.wait()
    all_codes = codes[...].astype(f32)
    codes_out[...] = all_codes
    row = row_ids((codes.shape[0], LANES))
    moved = []
    for m in range(2):
        source = jnp.max(jnp.where(codes_out[:, m, :] == me, row, 0))
        page_in = pltpu.make_async_copy(
            gathered.at[source, pl.ds(m * LANES, LANES), :], page.at[m], page_sem.at[m]
        )
        raw_in = pltpu.make_async_copy(
            gathered.at[source, pl.ds(2 * LANES, 64), pl.ds(m * LANES, LANES)],
            raw.at[m],
            raw_sem.at[m],
        )
        page_in.start()
        raw_in.start()
        moved.append((page_in, raw_in))
    stores = []
    for m in range(2):
        moved[m][0].wait()
        place = pool_out.at[pages[half, slots[0, m]]]
        stores.append(pltpu.make_async_copy(page.at[m], place, page_sem.at[2 + m]))
        stores[-1].start()
    for m in range(2):
        moved[m][1].wait()
        wide[m] = raw[m].astype(f32)
        place = memory_out.at[slots[0, m]]
        stores.append(pltpu.make_async_copy(wide.at[m], place, wide_sem.at[m]))
        stores[-1].start()
    for store in stores:
        store.wait()


def rows_kernel(rows_all, codes, rows_out, rows):
    del codes
    rows[...] = rows_all[...].astype(f32)
    for k in range(8):
        rows_out[:, k * LANES : (k + 1) * LANES] = rows[:, k, :].astype(bf16)


def body(
    tokens,
    lengths,
    prompt_group,
    span_close,
    out_slot,
    move_dest,
    page_table,
    cache_pool,
    prefix_cache,
    memory,
    norm_attn,
    norm_mlp,
    qkv_weight,
    out_weight,
    gate_weight,
    up_weight,
    down_weight,
    forget,
    write_rate,
):
    shape = jax.ShapeDtypeStruct
    rows = tokens.shape[0]
    n_tp = lax.axis_size("tp")
    n_rep = lax.axis_size("rep")
    pages = page_table.transpose(2, 1, 0)[0]
    pool = cache_pool[:, 0]
    prefix = prefix_cache[:, 0]
    mem = memory[:, 0]
    send_shape = shape((2 * LANES + 72, 2 * LANES), bf16)

    qkv_slots, kept, slices = call(
        qkv_kernel,
        (
            shape((n_tp, rows, LANES), bf16),
            shape((2, 8, LANES), f32),
            shape((rows, LANES), f32),
        ),
        [HBM] * 4,
        scratch=[
            pltpu.VMEM(tokens.shape, bf16),
            pltpu.VMEM((1, tokens.shape[1]), f32),
            pltpu.VMEM((4, qkv_weight.shape[1], qkv_weight.shape[0] // 4), bf16),
            pltpu.SemaphoreType.DMA((7,)),
        ],
    )(*in_hbm(tokens, norm_attn.reshape(1, -1), qkv_weight.T, norm_mlp.reshape(8, LANES)))
    qkv_recv = lax.all_to_all(qkv_slots, "tp", 0, 0)

    gate = gate_weight.T
    up = up_weight.T
    loaded = call(
        load_kernel,
        (
            shape((4, rows, LANES), jnp.int32),
            shape((8, LANES), jnp.int32),
            shape((8, LANES), f32),
            shape(pool.shape, bf16),
            shape(prefix.shape, bf16),
            shape(mem.shape, f32),
            shape(out_weight.shape, bf16),
            shape(gate.shape, bf16),
            shape(up.shape, bf16),
            shape(down_weight.shape, bf16),
            shape((2,) + mem.shape[1:], f32),
            send_shape,
        ),
        [HBM] * 15,
        out_specs=(VMEM,) * 11 + (HBM,),
        scratch=[
            pltpu.SMEM((rows,), jnp.int32),
            pltpu.SMEM((rows,), jnp.int32),
            pltpu.SMEM((rows,), jnp.int32),
            pltpu.SMEM(pages.shape, jnp.int32),
            pltpu.SMEM(out_slot.shape, jnp.int32),
            pltpu.SMEM(move_dest.shape, jnp.int32),
            pltpu.SMEM(forget.shape, f32),
            pltpu.SMEM(write_rate.shape, f32),
            pltpu.VMEM((8, 2 * LANES), bf16),
            pltpu.SemaphoreType.DMA((8,)),
            pltpu.SemaphoreType.DMA((7,)),
            pltpu.SemaphoreType.DMA((3,)),
        ],
    )(
        *in_hbm(lengths, prompt_group, span_close, pages, out_slot, move_dest, forget, write_rate),
        *in_hbm(pool, prefix, mem, out_weight, gate, up, down_weight),
    )

    columns, marks, rates, pool_near, prefix_near, mem_near = loaded[:6]
    out_near, gate_near, up_near, down_near, leaving_mem, send = loaded[6:]

    away, here, send = call(
        attend_kernel,
        (shape((rows, LANES), f32), shape((rows, LANES), f32), send_shape),
        [VMEM] * 7 + [HBM],
        out_specs=(VMEM, VMEM, HBM),
        scratch=[pltpu.VMEM((64, 2 * LANES), bf16), pltpu.SemaphoreType.DMA],
        aliases={7: 2},
    )(
        qkv_recv, columns, rates, marks, pool_near, prefix_near, leaving_mem, *in_hbm(send)
    )
    gathered = lax.all_gather(send, "rep", axis=0)
    away_recv = lax.ppermute(away, "tp", [(i, (i + n_tp // 2) % n_tp) for i in range(n_tp)])
    mem_after, recalled, pool_base = call(
        memory_kernel,
        (shape(mem.shape, f32), shape((rows, LANES), f32), shape(pool.shape, bf16)),
        [VMEM] * 5,
        out_specs=(VMEM, VMEM, HBM),
        scratch=[pltpu.VMEM((rows, rows * 64), f32), pltpu.SemaphoreType.DMA],
    )(qkv_recv, columns, rates, pool_near, mem_near)

    row_scratch = pltpu.VMEM((rows, 8, LANES), f32)
    mixed, leaving = call(
        join_kernel, (shape((rows, LANES), f32), shape((n_rep, 8, LANES), bf16)), [VMEM] * 5
    )(here, away_recv, recalled, slices, marks)
    arrived = lax.all_to_all(leaving, "rep", 0, 0)
    terms = call(
        project_kernel,
        shape((n_tp, 8, LANES), bf16),
        [VMEM] * 4,
        scratch=[row_scratch, pltpu.VMEM((n_rep, 8, LANES), f32)],
    )(mixed, arrived, marks, out_near)
    terms_recv = lax.all_to_all(terms, "tp", 0, 0)

    hidden, normed_slots = call(
        hidden_kernel,
        (shape((8, LANES), f32), shape((n_tp, 8, LANES), bf16)),
        [VMEM] * 3,
    )(terms_recv, kept, marks)
    normed_recv = lax.all_to_all(normed_slots, "tp", 0, 0)

    down_slots = call(
        mlp_kernel, shape((n_tp, 8, LANES), bf16), [VMEM] * 4, scratch=[row_scratch]
    )(normed_recv, gate_near, up_near, down_near)
    down_recv = lax.all_to_all(down_slots, "tp", 0, 0)

    row_slots = call(row_kernel, shape((n_tp, 8, LANES), bf16), [VMEM] * 2)(down_recv, hidden)
    rows_all = lax.all_to_all(row_slots, "tp", 0, 0)

    pool_out, mem_out, codes = call(
        place_kernel,
        (shape(pool.shape, bf16), shape(mem.shape, f32), shape((n_rep, 8, LANES), f32)),
        [HBM] * 5,
        out_specs=(HBM, HBM, VMEM),
        scratch=[
            pltpu.SMEM(pages.shape, jnp.int32),
            pltpu.SMEM(out_slot.shape, jnp.int32),
            pltpu.VMEM((n_rep, 8, LANES), bf16),
            pltpu.VMEM((2, LANES, 2 * LANES), bf16),
            pltpu.VMEM((2, 64, LANES), bf16),
            pltpu.VMEM((2, 64, LANES), f32),
            pltpu.SemaphoreType.DMA((3,)),
            pltpu.SemaphoreType.DMA((4,)),
            pltpu.SemaphoreType.DMA((2,)),
            pltpu.SemaphoreType.DMA((2,)),
        ],
        aliases={2: 0, 3: 1},
    )(*in_hbm(pages, out_slot, pool_base, mem_after, gathered))
    rows_out = call(
        rows_kernel, shape(tokens.shape, bf16), [VMEM] * 2, scratch=[row_scratch]
    )(rows_all, codes)
    return rows_out, mem_out[:, None], pool_out[:, None]


def solution(mesh):
    placed = (
        P("rep", None),
        P("rep"),
        P("rep"),
        P("rep"),
        P("rep", None),
        P("rep", None),
        P("rep", None, None),
        P("rep", "tp", None, None),
        P(None, "tp", None, None),
        P("rep", "tp", None, None),
        P(),
        P(),
        P(None, "tp"),
        P("tp", None),
        P(None, "tp"),
        P(None, "tp"),
        P("tp", None),
        P(),
        P(),
    )
    return jax.shard_map(
        body,
        mesh=mesh,
        in_specs=placed,
        out_specs=(P("rep", None), P("rep", "tp", None, None), P("rep", "tp", None, None)),
        check_vma=False,
    )
```
